256 devices in a mesh: grid: 64 (over z, y, core), snap: 4 (over x).
Axes of the slice: x: 4, y: 4, z: 8, core: 2. Of those that a mesh axis runs over, the one named last changes fastest.
Arguments:
- fields: bfloat16 [393216, 1024], P('grid', 'snap'), may hold values from -40 to 40
- start_local: float32 [1024, 128], P('snap'), may hold values from -6 to 6
- start_pair: float32 [2, 256, 128], replicated, may hold values from -6 to 6
- start_root: float32 [256, 128], replicated, may hold values from -6 to 6
Outputs:
- modes: bfloat16 [393216, 128], P(('grid', 'snap'))
The draws below stay inside these ranges and needn't reach their ends.
All inputs are finite; a program needn't handle non-finite values.
Results may differ from the reference program's by a relative error of at most 0.0055.
Values may be sent and summed in bfloat16 or wider, within the bound.
A program may use at most 64 MiB of HBM per device.

```python
import math
import jax
import jax.numpy as jnp
from jax import lax

ROWS_DEV = 6144
SNAP_DEV = 256
RANK = 128
POWER = 2
NEWTON = 8
MODES = 24
POINTS = 393216
SNAPS = 1024
N_GRID = 64
N_SNAP = 4


def draw_fields(key, part):
    subkeys = jax.random.split(jax.random.fold_in(key, 11), 7)
    regions = 4 * N_GRID
    region_rows = ROWS_DEV // 4
    envelope = jnp.exp(jax.random.uniform(subkeys[0], (regions, MODES), jnp.float32, math.log(0.1), math.log(3.0)))
    spatial = jax.random.normal(subkeys[1], (regions, region_rows, MODES), jnp.float32) * envelope[:, None, :]
    amplitude = 3.0 * 0.8 ** jnp.arange(MODES, dtype=jnp.float32)
    spatial = spatial.reshape(POINTS, MODES) * amplitude
    temporal = jax.random.normal(subkeys[2], (MODES, SNAPS), jnp.float32)
    signal = jnp.dot(spatial, temporal, precision=lax.Precision.HIGHEST)
    ramp = jnp.arange(N_GRID, dtype=jnp.float32) / max(N_GRID - 1, 1)
    local_scale = 0.4 * math.sqrt(N_GRID) * jnp.exp(ramp * math.log(3.0))
    local_space = jax.random.normal(subkeys[5], (N_GRID, ROWS_DEV, 2), jnp.float32) * local_scale[:, None, None]
    local_time = jax.random.normal(subkeys[6], (N_GRID, 2, SNAPS), jnp.float32)
    local_part = jnp.matmul(local_space, local_time, precision=lax.Precision.HIGHEST).reshape(POINTS, SNAPS)
    noise_part = jax.random.normal(subkeys[4], (POINTS, SNAPS), jnp.float32)
    return jnp.clip(signal + local_part + noise_part, -40.0, 40.0).astype(jnp.bfloat16)


def block_scale(own_key, extent, shards, low, largest):
    def one(dim, blocks):
        steps = jax.random.uniform(jax.random.fold_in(jax.random.fold_in(own_key, 6), dim), (blocks,), jnp.float32, low / len(shards), largest / len(shards))
        return jnp.repeat(jnp.exp(steps), extent[dim] // blocks).reshape((-1,) + (1,) * (len(extent) - dim - 1))

    factor_of = one(*shards[0])
    for cut in shards[1:]:
        factor_of = factor_of * one(*cut)
    return factor_of


def normal_values(key, shape, scale, most, shards=(), kind=jnp.bfloat16):
    array = jax.random.normal(key, shape, jnp.float32) * scale
    if len(shards) > 0:
        array = block_scale(key, shape, shards, -0.22, 0.18) * array
    return jnp.clip(array, min=-most, max=most).astype(kind)


def setup_inputs(seed: int = 0) -> dict:
    key_list = jax.random.split(jax.random.key(seed), 5)
    return {
        "fields": draw_fields(jax.random.fold_in(key_list[4], 71), 0),
        "start_local": normal_values(key_list[1], (SNAPS, RANK), 1.0, 6.0, ((0, 4),), jnp.float32),
        "start_pair": normal_values(key_list[2], (2, 2 * RANK, RANK), 1.0, 6.0, (), jnp.float32),
        "start_root": normal_values(key_list[3], (2 * RANK, RANK), 1.0, 6.0, (), jnp.float32),
    }


def polar_basis(gram_matrix, initial):
    current = initial
    for power_step in range(POWER):
        product = jnp.dot(gram_matrix, current, precision=lax.Precision.HIGHEST)
        iterate = product / jnp.sqrt(jnp.sum(product * product) + 1e-06)
        for newton_step in range(NEWTON):
            inner_gram = jnp.dot(iterate.T, iterate, precision=lax.Precision.HIGHEST)
            iterate = 1.5 * iterate - 0.5 * jnp.dot(iterate, inner_gram, precision=lax.Precision.HIGHEST)
        current = iterate
    return current

def reference(fields, start_local, start_pair, start_root):
    inverse_count = 1.0 / POINTS
    leaves = []
    for column_block in range(N_SNAP):
        columns = fields[:, column_block * SNAP_DEV:(column_block + 1) * SNAP_DEV]
        gram_sum = jnp.dot(columns.T, columns, preferred_element_type=jnp.float32) * inverse_count
        rotation = polar_basis(gram_sum, start_local[column_block * SNAP_DEV:(column_block + 1) * SNAP_DEV])
        leaves.append(jnp.dot(columns, rotation.astype(jnp.bfloat16), preferred_element_type=jnp.float32).astype(jnp.bfloat16))
    merged = []
    for pair_index in range(2):
        joined = jnp.concatenate([leaves[2 * pair_index], leaves[2 * pair_index + 1]], axis=1)
        gram_sum = jnp.dot(joined.T, joined, preferred_element_type=jnp.float32) * inverse_count
        rotation = polar_basis(gram_sum, start_pair[pair_index])
        merged.append(jnp.dot(joined, rotation.astype(jnp.bfloat16), preferred_element_type=jnp.float32).astype(jnp.bfloat16))
    joined = jnp.concatenate(merged, axis=1)
    gram_sum = jnp.dot(joined.T, joined, preferred_element_type=jnp.float32) * inverse_count
    rotation = polar_basis(gram_sum, start_root)
    return jnp.dot(joined, rotation.astype(jnp.bfloat16), preferred_element_type=jnp.float32).astype(jnp.bfloat16)
```

```python
import functools

import jax
import jax.numpy as jnp
from jax import lax
from jax.experimental import pallas as pl
from jax.experimental.pallas import tpu as pltpu
from jax.sharding import Mesh
from jax.sharding import PartitionSpec as P

POWER = 2
NEWTON = 8
RANK = 128
NZ, NY, NC, NX = 8, 4, 2, 4
ROW = NY * NC
PLANE = NX * ROW
MESH = pl.DeviceIdType.MESH
F32 = jnp.float32
BF16 = jnp.bfloat16


def exact(a, b):
    return jnp.dot(a, b, precision=lax.Precision.HIGHEST, preferred_element_type=F32)


def product(a, b):
    return jnp.dot(a, b, preferred_element_type=F32)


def product_t(a, b):
    return lax.dot_general(a, b, (((0,), (0,)), ((), ())), preferred_element_type=F32)


def power_step(gram, basis):
    step = exact(gram, basis)
    z = step * (1.0 / jnp.sqrt(jnp.sum(step * step) + 1e-06))
    for _ in range(NEWTON):
        z = 1.5 * z - 0.5 * exact(z, exact(z.T, z))
    return z


def body(
    inverse_count,
    fields, start_local, start_pair, start_root,
    out,
    f, s_local, s_pair, s_root,
    gram, got_a, part_b, got_b, mine_c, col_c, full_d,
    leaves, sent_leaf, diag, diag_part, diag_all,
    pair_part, got_p, mine_p, zs_p, pair_all, piece_p,
    cross_part, got_x, mine_x, zs_x, cross_all, piece_x,
    load_sem, start_sem, a_sem, b_sem, c_sem, d_sem, leaf_sem, e_sem, g_sem, p_sem, x_sem,
):
    z, y, c, x = (lax.axis_index(name) for name in ("z", "y", "c", "x"))
    j = y * NC + c
    t = x * ROW + j
    quarter = f.shape[0] // NX

    def send(src, dst, sems, **where):
        pltpu.make_async_remote_copy(
            src_ref=src, dst_ref=dst, send_sem=sems.at[0], recv_sem=sems.at[1],
            device_id=where, device_id_type=MESH,
        ).start()

    def await_bytes(ref, sem):
        pltpu.make_async_copy(ref, ref, sem).wait()

    def in_row(d):
        peer = lax.rem(j + d, ROW)
        return peer, dict(y=peer // NC, c=lax.rem(peer, NC))

    def in_plane(d):
        peer = lax.rem(t + d, PLANE)
        return peer, dict(x=peer // ROW, y=lax.rem(peer // NC, NY), c=lax.rem(peer, NC))

    for k in range(NX):
        rows = pl.ds(k * quarter, quarter)
        pltpu.make_async_copy(fields.at[rows], f.at[rows], load_sem.at[k]).start()
    starts = [(start_local, s_local), (start_pair, s_pair), (start_root, s_root)]
    for k, (src, dst) in enumerate(starts):
        pltpu.make_async_copy(src, dst, start_sem.at[k]).start()

    barrier = pltpu.get_barrier_semaphore()

    @pl.loop(1, PLANE)
    def _(d):
        pl.semaphore_signal(barrier, inc=1, device_id=in_plane(d)[1], device_id_type=MESH)

    @pl.loop(1, NZ)
    def _(d):
        pl.semaphore_signal(barrier, inc=1, device_id=dict(z=lax.rem(z + d, NZ)), device_id_type=MESH)

    total = None
    for k in range(NX):
        rows = pl.ds(k * quarter, quarter)
        pltpu.make_async_copy(fields.at[rows], f.at[rows], load_sem.at[k]).wait()
        part = f[rows]
        term = product_t(part, part)
        total = term if total is None else total + term
    gram[...] = total
    pl.semaphore_wait(barrier, PLANE - 1 + NZ - 1)

    strip = gram.shape[0] // ROW

    @pl.loop(1, ROW)
    def _(d):
        peer, where = in_row(d)
        send(gram.at[pl.ds(pl.multiple_of(peer * strip, 8), strip)], got_a.at[d - 1], a_sem, **where)

    await_bytes(got_a, a_sem.at[1])
    sums = gram[pl.ds(pl.multiple_of(j * strip, 8), strip)] + got_a[...].sum(axis=0)
    for k in range(NZ):
        part_b[k] = sums[8 * (k // 2):8 * (k // 2) + 8, 128 * (k % 2):128 * (k % 2) + 128]

    @pl.loop(1, NZ)
    def _(d):
        peer = lax.rem(z + d, NZ)
        send(part_b.at[peer], got_b.at[d - 1], b_sem, z=peer)

    await_bytes(got_b, b_sem.at[1])
    tile = part_b[z] + got_b[...].sum(axis=0)
    mine_c[...] = tile
    col_c[z] = tile

    @pl.loop(1, NZ)
    def _(d):
        send(mine_c, col_c.at[z], c_sem, z=lax.rem(z + d, NZ))

    await_bytes(got_b, c_sem.at[1])
    full_d[j] = col_c[...]

    @pl.loop(1, ROW)
    def _(d):
        send(col_c, full_d.at[j], d_sem, **in_row(d)[1])

    await_bytes(full_d.at[pl.ds(0, ROW - 1)], d_sem.at[1])
    whole = jnp.concatenate(
        [
            jnp.concatenate([full_d[n, 2 * k], full_d[n, 2 * k + 1]], axis=1)
            for n in range(ROW)
            for k in range(NZ // 2)
        ],
        axis=0,
    ) * inverse_count

    for k, (src, dst) in enumerate(starts):
        pltpu.make_async_copy(src, dst, start_sem.at[k]).wait()
    basis = s_local[...]
    for _ in range(POWER):
        basis = power_step(whole, basis)
    rotation = basis.astype(BF16)

    for n, d in enumerate((2, 1, 3)):
        peer = lax.rem(x + d, NX)
        rows = pl.ds(pl.multiple_of(peer * quarter, quarter), quarter)
        sent_leaf[n] = product(f[rows], rotation).astype(BF16)
        send(sent_leaf.at[n], leaves.at[x], leaf_sem, x=peer)

    wide = rotation.astype(F32)
    diag[...] = exact(wide.T, exact(whole, wide))
    part16 = pl.ds(pl.multiple_of(j * 16, 16), 16)
    diag_part[x] = diag[part16]

    for d in (1, 2, 3):
        send(diag.at[part16], diag_part.at[x], e_sem, x=lax.rem(x + d, NX))

    own = pl.ds(pl.multiple_of(x * quarter, quarter), quarter)
    leaves[x] = product(f[own], rotation).astype(BF16)
    await_bytes(diag_part.at[pl.ds(0, NX - 1)], e_sem.at[1])
    diag_all[j] = diag_part[...]

    @pl.loop(1, ROW)
    def _(d):
        send(diag_part, diag_all.at[j], g_sem, **in_row(d)[1])

    await_bytes(leaves.at[pl.ds(0, NX - 1)], leaf_sem.at[1])

    pair_part[0:128] = product_t(leaves[0], leaves[1])
    pair_part[128:256] = product_t(leaves[2], leaves[3])

    @pl.loop(1, PLANE)
    def _(d):
        peer, where = in_plane(d)
        send(pair_part.at[pl.ds(pl.multiple_of(peer * 8, 8), 8)], got_p.at[d - 1], p_sem.at[0], **where)

    left = jnp.concatenate([leaves[0], leaves[1]], axis=1)
    right = jnp.concatenate([leaves[2], leaves[3]], axis=1)
    cross_part[...] = product_t(left, right)

    @pl.loop(1, PLANE)
    def _(d):
        peer, where = in_plane(d)
        send(cross_part.at[pl.ds(pl.multiple_of(peer * 8, 8), 8)], got_x.at[d - 1], x_sem.at[0], **where)

    my8 = pl.ds(pl.multiple_of(t * 8, 8), 8)

    def over_z(got, part, mine, zs, sems):
        await_bytes(got, sems.at[0, 1])
        value = part[my8] + got[...].sum(axis=0)
        mine[...] = value
        zs[z] = value

        @pl.loop(1, NZ)
        def _(d):
            send(mine, zs.at[z], sems.at[1], z=lax.rem(z + d, NZ))

    def to_plane(zs, piece, whole_ref, sems):
        await_bytes(zs.at[pl.ds(0, NZ - 1)], sems.at[1, 1])
        value = zs[...].sum(axis=0) * inverse_count
        piece[...] = value
        whole_ref[my8] = value

        @pl.loop(1, PLANE)
        def _(d):
            send(piece, whole_ref.at[my8], sems.at[2], **in_plane(d)[1])

    def from_plane(whole_ref, sems):
        await_bytes(whole_ref.at[pl.ds(0, 8 * (PLANE - 1))], sems.at[2, 1])

    over_z(got_p, pair_part, mine_p, zs_p, p_sem)
    to_plane(zs_p, piece_p, pair_all, p_sem)
    over_z(got_x, cross_part, mine_x, zs_x, x_sem)
    await_bytes(diag_all.at[pl.ds(0, ROW - 1)], g_sem.at[1])
    diags = [jnp.concatenate([diag_all[n, b] for n in range(ROW)], axis=0) for b in range(NX)]
    from_plane(pair_all, p_sem)

    def pair_gram(n):
        block = pair_all[128 * n:128 * n + 128]
        top = jnp.concatenate([diags[2 * n], block], axis=1)
        low = jnp.concatenate([block.T, diags[2 * n + 1]], axis=1)
        return jnp.concatenate([top, low], axis=0)

    grams = [pair_gram(0), pair_gram(1)]
    bases = [power_step(grams[n], s_pair[n]) for n in range(2)]
    to_plane(zs_x, piece_x, cross_all, x_sem)
    bases = [power_step(grams[n], bases[n]) for n in range(2)]
    rotations = [basis.astype(BF16) for basis in bases]
    wides = [r.astype(F32) for r in rotations]
    branch = jnp.concatenate(
        [product(left, rotations[0]).astype(BF16), product(right, rotations[1]).astype(BF16)], axis=1
    )
    first = exact(wides[0].T, exact(grams[0], wides[0]))
    second = exact(wides[1].T, exact(grams[1], wides[1]))
    from_plane(cross_all, x_sem)
    mixed = exact(wides[0].T, exact(cross_all[...], wides[1]))
    root_gram = jnp.concatenate(
        [jnp.concatenate([first, mixed], axis=1), jnp.concatenate([mixed.T, second], axis=1)], axis=0
    )
    basis = s_root[...]
    for _ in range(POWER):
        basis = power_step(root_gram, basis)
    out[...] = product(branch, basis.astype(BF16)).astype(BF16)

    await_bytes(got_a, a_sem.at[0])
    await_bytes(got_b, b_sem.at[0])
    await_bytes(got_b, c_sem.at[0])
    await_bytes(full_d.at[pl.ds(0, ROW - 1)], d_sem.at[0])
    await_bytes(sent_leaf, leaf_sem.at[0])
    await_bytes(diag_part.at[pl.ds(0, NX - 1)], e_sem.at[0])
    await_bytes(diag_all.at[pl.ds(0, ROW - 1)], g_sem.at[0])
    for got, zs, whole_ref, sems in ((got_p, zs_p, pair_all, p_sem), (got_x, zs_x, cross_all, x_sem)):
        await_bytes(got, sems.at[0, 0])
        await_bytes(zs.at[pl.ds(0, NZ - 1)], sems.at[1, 0])
        await_bytes(whole_ref.at[pl.ds(0, 8 * (PLANE - 1))], sems.at[2, 0])


def on_device(points, fields, start_local, start_pair, start_root):
    rows, snaps = fields.shape
    vmem = pltpu.VMEM
    dma = pltpu.SemaphoreType.DMA
    quarter = rows // NX
    scratch = [
        vmem((rows, snaps), BF16), vmem(start_local.shape, F32), vmem(start_pair.shape, F32), vmem(start_root.shape, F32),
        vmem((snaps, snaps), F32), vmem((ROW - 1, snaps // ROW, snaps), F32), vmem((NZ, 8, 128), F32),
        vmem((NZ - 1, 8, 128), F32), vmem((8, 128), F32), vmem((NZ, 8, 128), F32), vmem((ROW, NZ, 8, 128), F32),
        vmem((NX, quarter, RANK), BF16), vmem((NX - 1, quarter, RANK), BF16), vmem((RANK, RANK), F32),
        vmem((NX, 16, RANK), F32), vmem((ROW, NX, 16, RANK), F32),
        vmem((256, 128), F32), vmem((PLANE - 1, 8, 128), F32), vmem((8, 128), F32), vmem((NZ, 8, 128), F32),
        vmem((256, 128), F32), vmem((8, 128), F32),
        vmem((256, 256), F32), vmem((PLANE - 1, 8, 256), F32), vmem((8, 256), F32), vmem((NZ, 8, 256), F32),
        vmem((256, 256), F32), vmem((8, 256), F32),
        dma((NX,)), dma((3,)), dma((2,)), dma((2,)), dma((2,)), dma((2,)), dma((2,)), dma((2,)), dma((2,)),
        dma((3, 2)), dma((3, 2)),
    ]
    anywhere = pl.BlockSpec(memory_space=pl.ANY)
    return pl.pallas_call(
        functools.partial(body, 1.0 / points),
        out_shape=jax.ShapeDtypeStruct((quarter, RANK), BF16),
        in_specs=[anywhere] * 4,
        out_specs=pl.BlockSpec(memory_space=pltpu.VMEM),
        scratch_shapes=scratch,
        compiler_params=pltpu.CompilerParams(
            collective_id=0, has_side_effects=True, vmem_limit_bytes=48 * 2**20
        ),
        name="snapshot_modes",
    )(fields, start_local, start_pair, start_root)


def solution(mesh):
    split = Mesh(mesh.devices.reshape(NZ, NY, NC, mesh.shape["snap"]), ("z", "y", "c", "x"))
    grid = ("z", "y", "c")

    def whole(fields, start_local, start_pair, start_root):
        return jax.shard_map(
            functools.partial(on_device, fields.shape[0]),
            mesh=split,
            in_specs=(P(grid, "x"), P("x", None), P(), P()),
            out_specs=P((*grid, "x"), None),
            check_vma=False,
        )(fields, start_local, start_pair, start_root)

    return whole
```

```python
import functools

import jax
import jax.numpy as jnp
from jax import lax
from jax.experimental import pallas as pl
from jax.experimental.pallas import tpu as pltpu
from jax.sharding import Mesh
from jax.sharding import PartitionSpec as P

POWER = 2
NEWTON = 8
RANK = 128
NZ, NY, NC, NX = 8, 4, 2, 4
ROW = NY * NC
SHEET = NZ * NY
PLANE = NX * ROW
EARLY = 3
PIECE = 384
MESH = pl.DeviceIdType.MESH
F32 = jnp.float32
BF16 = jnp.bfloat16


def product(a, b):
    return jnp.dot(a, b, preferred_element_type=F32)


def product_t(a, b):
    return lax.dot_general(a, b, (((0,), (0,)), ((), ())), preferred_element_type=F32)


def halves(a):
    high = a.astype(BF16)
    return high, (a - high.astype(F32)).astype(BF16)


def three_products(a, b, dims):
    (a_high, a_low), (b_high, b_low) = halves(a), halves(b)
    (a_dim,), (b_dim,) = dims
    left = jnp.concatenate([a_high, a_high, a_low], axis=a_dim)
    right = jnp.concatenate([b_high, b_low, b_high], axis=b_dim)
    return lax.dot_general(left, right, (dims, ((), ())), preferred_element_type=F32)


def power_steps(grams, bases):
    steps = [three_products(basis, gram, ((1,), (0,))) for gram, basis in zip(grams, bases)]
    flat = [w * (1.0 / jnp.sqrt(jnp.sum(w * w) + 1e-06)) for w in steps]
    for _ in range(NEWTON):
        inner = [three_products(w, w, ((1,), (1,))) for w in flat]
        flat = [1.5 * w - 0.5 * three_products(s, w, ((1,), (0,))) for s, w in zip(inner, flat)]
    return flat


def turned(gram, left, right):
    high, low = halves(gram)
    middle = product(jnp.concatenate([high, low], axis=1), jnp.concatenate([right, right], axis=0))
    high, low = halves(middle)
    return product_t(jnp.concatenate([left, left], axis=0), jnp.concatenate([high, low], axis=0))


def body(
    inverse_count,
    fields, start_local, start_pair, start_root,
    out,
    f, s_local, s_pair, s_root,
    gram, got_c, part_a, got_a, mine_a, col,
    raw, rot_all, leaves, sent_leaf, diag, diag_part, diag_all,
    pair_part, got_p, mine_p, zs_p, pair_all, piece_p,
    cross_part, got_x, mine_x, zs_x, cross_all, piece_x,
    load_sem, start_sem, c_sem, a_sem, b_sem, d_sem, raw_sem, rot_sem, leaf_sem, e_sem, g_sem, p_sem, x_sem,
):
    z, y, c, x = (lax.axis_index(name) for name in ("z", "y", "c", "x"))
    j = y * NC + c
    m = z * NY + y
    t = x * ROW + j
    quarter = f.shape[0] // NX
    early = raw.shape[1]
    late = quarter - early
    pending = []

    def send(src, dst, sems, **where):
        pltpu.make_async_remote_copy(
            src_ref=src, dst_ref=dst, send_sem=sems.at[0], recv_sem=sems.at[1],
            device_id=where, device_id_type=MESH,
        ).start()

    def await_bytes(ref, sem):
        pltpu.make_async_copy(ref, ref, sem).wait()

    def arrived(ref, sems):
        pending.append((ref, sems.at[0]))
        await_bytes(ref, sems.at[1])

    def greet(**where):
        pl.semaphore_signal(pltpu.get_barrier_semaphore(), inc=1, device_id=where, device_id_type=MESH)

    def in_row(d):
        peer = lax.rem(j + d, ROW)
        return peer, dict(y=peer // NC, c=lax.rem(peer, NC))

    def in_sheet(d):
        peer = lax.rem(m + d, SHEET)
        return peer, dict(z=peer // NY, y=lax.rem(peer, NY))

    def in_plane(d):
        peer = lax.rem(t + d, PLANE)
        return peer, dict(x=peer // ROW, y=lax.rem(peer // NC, NY), c=lax.rem(peer, NC))

    loads = []
    for k in range(NX):
        rows = pl.ds(k * quarter, quarter)
        loads.append(pltpu.make_async_copy(fields.at[rows], f.at[rows], load_sem.at[k]))
    own_early = pl.ds(pl.multiple_of(x * quarter, quarter), early)
    loads.append(pltpu.make_async_copy(fields.at[own_early], raw.at[x], load_sem.at[NX]))
    for k, (src, dst) in enumerate([(start_local, s_local), (start_pair, s_pair), (start_root, s_root)]):
        loads.append(pltpu.make_async_copy(src, dst, start_sem.at[k]))
    for load in loads:
        load.start()

    @pl.loop(1, SHEET)
    def _(d):
        greet(**in_sheet(d)[1])

    greet(c=1 - c)
    for d in range(1, NX):
        greet(x=lax.rem(x + d, NX))

    total = None
    for k in range(NX):
        loads[k].wait()
        part = f[pl.ds(k * quarter, quarter)]
        term = product_t(part, part)
        total = term if total is None else total + term
    gram[...] = total
    pl.semaphore_wait(pltpu.get_barrier_semaphore(), SHEET - 1 + 1 + NX - 1)

    half = gram.shape[0] // NC
    send(gram.at[pl.ds(pl.multiple_of((1 - c) * half, 8), half)], got_c, c_sem, c=1 - c)

    @pl.loop(0, early // PIECE)
    def _(k):
        for d in (2, 1, 3):
            peer = lax.rem(x + d, NX)
            rows = pl.ds(pl.multiple_of(peer * quarter + k * PIECE, PIECE), PIECE)
            send(f.at[rows], raw.at[x, pl.ds(pl.multiple_of(k * PIECE, PIECE), PIECE)], raw_sem, x=peer)

    arrived(got_c, c_sem)
    kept = gram[pl.ds(pl.multiple_of(c * half, 8), half)] + got_c[...]
    for n in range(SHEET):
        r, s = 8 * (n // 2), 128 * (n % 2)
        part_a[n] = kept[r:r + 8, s:s + 128]

    @pl.loop(1, SHEET)
    def _(d):
        peer, where = in_sheet(d)
        send(part_a.at[peer], got_a.at[d - 1], a_sem, **where)

    arrived(got_a, a_sem)
    tile = (part_a[m] + got_a[...].sum(axis=0)) * inverse_count
    mine_a[...] = tile
    col[c, m] = tile

    @pl.loop(1, SHEET)
    def _(d):
        send(mine_a, col.at[c, m], b_sem, **in_sheet(d)[1])

    arrived(col.at[0, pl.ds(0, SHEET - 1)], b_sem)
    send(col.at[c], col.at[c], d_sem, c=1 - c)
    arrived(col.at[0], d_sem)
    whole = jnp.concatenate(
        [
            jnp.concatenate([col[n, 2 * k], col[n, 2 * k + 1]], axis=1)
            for n in range(NC)
            for k in range(SHEET // 2)
        ],
        axis=0,
    )
    for load in loads[NX:]:
        load.wait()
    bases = [s_local[...].T]
    for _ in range(POWER):
        bases = power_steps([whole], bases)
    rotation = bases[0].T.astype(BF16)

    rot_all[x] = rotation
    for d in (2, 1, 3):
        send(rot_all.at[x], rot_all.at[x], rot_sem, x=lax.rem(x + d, NX))
    for n, d in enumerate((2, 1, 3)):
        peer = lax.rem(x + d, NX)
        rows = pl.ds(pl.multiple_of(peer * quarter + early, PIECE), late)
        sent_leaf[n] = product(f[rows], rotation).astype(BF16)
        send(sent_leaf.at[n], leaves.at[x, pl.ds(early, late)], leaf_sem, x=peer)

    diag[...] = turned(whole, rotation, rotation)
    part16 = pl.ds(pl.multiple_of(j * 16, 16), 16)
    diag_part[x] = diag[part16]
    for d in (1, 2, 3):
        send(diag.at[part16], diag_part.at[x], e_sem, x=lax.rem(x + d, NX))

    own_late = pl.ds(pl.multiple_of(x * quarter + early, PIECE), late)
    leaves[x, pl.ds(early, late)] = product(f[own_late], rotation).astype(BF16)

    arrived(raw.at[pl.ds(0, NX - 1)], raw_sem)
    arrived(rot_all.at[pl.ds(0, NX - 1)], rot_sem)
    for b in range(NX):
        leaves[b, pl.ds(0, early)] = product(raw[b], rot_all[b]).astype(BF16)
    arrived(leaves.at[pl.ds(0, NX - 1), pl.ds(early, late)], leaf_sem)

    pair_part[0:128] = product_t(leaves[0], leaves[1])
    pair_part[128:256] = product_t(leaves[2], leaves[3])

    @pl.loop(1, PLANE)
    def _(d):
        peer, where = in_plane(d)
        send(pair_part.at[pl.ds(pl.multiple_of(peer * 8, 8), 8)], got_p.at[d - 1], p_sem.at[0], **where)

    left = jnp.concatenate([leaves[0], leaves[1]], axis=1)
    right = jnp.concatenate([leaves[2], leaves[3]], axis=1)
    cross_part[...] = product_t(left, right)

    @pl.loop(1, PLANE)
    def _(d):
        peer, where = in_plane(d)
        send(cross_part.at[pl.ds(pl.multiple_of(peer * 8, 8), 8)], got_x.at[d - 1], x_sem.at[0], **where)

    arrived(diag_part.at[pl.ds(0, NX - 1)], e_sem)
    diag_all[j] = diag_part[...]

    @pl.loop(1, ROW)
    def _(d):
        send(diag_part, diag_all.at[j], g_sem, **in_row(d)[1])

    my8 = pl.ds(pl.multiple_of(t * 8, 8), 8)

    def over_z(got, part, mine, zs, sems):
        arrived(got, sems.at[0])
        value = part[my8] + got[...].sum(axis=0)
        mine[...] = value
        zs[z] = value

        @pl.loop(1, NZ)
        def _(d):
            send(mine, zs.at[z], sems.at[1], z=lax.rem(z + d, NZ))

    def to_plane(zs, piece, whole_ref, sems):
        arrived(zs.at[pl.ds(0, NZ - 1)], sems.at[1])
        value = zs[...].sum(axis=0) * inverse_count
        piece[...] = value
        whole_ref[my8] = value

        @pl.loop(1, PLANE)
        def _(d):
            send(piece, whole_ref.at[my8], sems.at[2], **in_plane(d)[1])

    def from_plane(whole_ref, sems):
        arrived(whole_ref.at[pl.ds(0, 8 * (PLANE - 1))], sems.at[2])

    over_z(got_p, pair_part, mine_p, zs_p, p_sem)
    to_plane(zs_p, piece_p, pair_all, p_sem)
    over_z(got_x, cross_part, mine_x, zs_x, x_sem)
    arrived(diag_all.at[pl.ds(0, ROW - 1)], g_sem)
    diags = [jnp.concatenate([diag_all[n, b] for n in range(ROW)], axis=0) for b in range(NX)]
    from_plane(pair_all, p_sem)

    def pair_gram(n):
        block = pair_all[128 * n:128 * n + 128]
        top = jnp.concatenate([diags[2 * n], block], axis=1)
        low = jnp.concatenate([block.T, diags[2 * n + 1]], axis=1)
        return jnp.concatenate([top, low], axis=0)

    grams = [pair_gram(0), pair_gram(1)]
    bases = power_steps(grams, [s_pair[n].T for n in range(2)])
    to_plane(zs_x, piece_x, cross_all, x_sem)
    bases = power_steps(grams, bases)
    rotations = [basis.T.astype(BF16) for basis in bases]
    first = turned(grams[0], rotations[0], rotations[0])
    second = turned(grams[1], rotations[1], rotations[1])
    from_plane(cross_all, x_sem)
    mixed = turned(cross_all[...], rotations[0], rotations[1])
    root_gram = jnp.concatenate(
        [jnp.concatenate([first, mixed], axis=1), jnp.concatenate([mixed.T, second], axis=1)], axis=0
    )
    bases = [s_root[...].T]
    for _ in range(POWER):
        bases = power_steps([root_gram], bases)
    branch = jnp.concatenate(
        [product(left, rotations[0]).astype(BF16), product(right, rotations[1]).astype(BF16)], axis=1
    )
    out[...] = product(branch, bases[0].T.astype(BF16)).astype(BF16)

    for ref, sem in pending:
        await_bytes(ref, sem)


def on_device(points, fields, start_local, start_pair, start_root):
    rows, snaps = fields.shape
    vmem = pltpu.VMEM
    dma = pltpu.SemaphoreType.DMA
    quarter = rows // NX
    early = EARLY * quarter // 4
    scratch = [
        vmem((rows, snaps), BF16), vmem(start_local.shape, F32), vmem(start_pair.shape, F32), vmem(start_root.shape, F32),
        vmem((snaps, snaps), F32), vmem((snaps // NC, snaps), F32), vmem((SHEET, 8, 128), F32),
        vmem((SHEET - 1, 8, 128), F32), vmem((8, 128), F32), vmem((NC, SHEET, 8, 128), F32),
        vmem((NX, early, snaps), BF16), vmem((NX, snaps, RANK), BF16),
        vmem((NX, quarter, RANK), BF16), vmem((NX - 1, quarter - early, RANK), BF16), vmem((RANK, RANK), F32),
        vmem((NX, 16, RANK), F32), vmem((ROW, NX, 16, RANK), F32),
        vmem((256, 128), F32), vmem((PLANE - 1, 8, 128), F32), vmem((8, 128), F32), vmem((NZ, 8, 128), F32),
        vmem((256, 128), F32), vmem((8, 128), F32),
        vmem((256, 256), F32), vmem((PLANE - 1, 8, 256), F32), vmem((8, 256), F32), vmem((NZ, 8, 256), F32),
        vmem((256, 256), F32), vmem((8, 256), F32),
        dma((NX + 1,)), dma((3,)), *[dma((2,))] * 9, dma((3, 2)), dma((3, 2)),
    ]
    anywhere = pl.BlockSpec(memory_space=pltpu.HBM)
    return pl.pallas_call(
        functools.partial(body, 1.0 / points),
        out_shape=jax.ShapeDtypeStruct((quarter, RANK), BF16),
        in_specs=[anywhere] * 4,
        out_specs=pl.BlockSpec(memory_space=pltpu.VMEM),
        scratch_shapes=scratch,
        compiler_params=pltpu.CompilerParams(
            collective_id=0, has_side_effects=True, vmem_limit_bytes=60 * 2**20
        ),
        name="snapshot_modes",
    )(fields, start_local, start_pair, start_root)


def solution(mesh):
    split = Mesh(mesh.devices.reshape(NZ, NY, NC, mesh.shape["snap"]), ("z", "y", "c", "x"))
    grid = ("z", "y", "c")

    def whole(fields, start_local, start_pair, start_root):
        return jax.shard_map(
            functools.partial(on_device, fields.shape[0]),
            mesh=split,
            in_specs=(P(grid, "x"), P("x", None), P(), P()),
            out_specs=P((*grid, "x"), None),
            check_vma=False,
        )(fields, start_local, start_pair, start_root)

    return whole
```

```python
import functools

import jax
import jax.numpy as jnp
from jax import lax
from jax.experimental import pallas as pl
from jax.experimental.pallas import tpu as pltpu
from jax.sharding import Mesh
from jax.sharding import PartitionSpec as P

POWER = 2
NEWTON = 8
RANK = 128
NZ, NY, NC, NX = 8, 4, 2, 4
ROW = NY * NC
SHEET = NZ * NY
PLANE = NX * ROW
EARLY = 6
PIECE = 192
MESH = pl.DeviceIdType.MESH
F32 = jnp.float32
BF16 = jnp.bfloat16


def product(a, b):
    return jnp.dot(a, b, preferred_element_type=F32)


def product_t(a, b):
    return lax.dot_general(a, b, (((0,), (0,)), ((), ())), preferred_element_type=F32)


def halves(a):
    high = a.astype(BF16)
    return high, (a - high.astype(F32)).astype(BF16)


def three_products(a, b, dims):
    (a_high, a_low), (b_high, b_low) = halves(a), halves(b)
    (a_dim,), (b_dim,) = dims
    left = jnp.concatenate([a_high, a_high, a_low], axis=a_dim)
    right = jnp.concatenate([b_high, b_low, b_high], axis=b_dim)
    return lax.dot_general(left, right, (dims, ((), ())), preferred_element_type=F32)


def power_steps(grams, bases):
    steps = [three_products(basis, gram, ((1,), (0,))) for gram, basis in zip(grams, bases)]
    flat = [w * (1.0 / jnp.sqrt(jnp.sum(w * w) + 1e-06)) for w in steps]
    for _ in range(NEWTON):
        inner = [three_products(w, w, ((1,), (1,))) for w in flat]
        flat = [1.5 * w - 0.5 * three_products(s, w, ((1,), (0,))) for s, w in zip(inner, flat)]
    return flat


def turned(gram, left, right):
    high, low = halves(gram)
    middle = product(jnp.concatenate([high, low], axis=1), jnp.concatenate([right, right], axis=0))
    high, low = halves(middle)
    return product_t(jnp.concatenate([left, left], axis=0), jnp.concatenate([high, low], axis=0))


def body(
    inverse_count,
    fields, start_local, start_pair, start_root,
    out,
    f, s_local, s_pair, s_root,
    gram, got_c, kept_y, got_y, part_a, got_a, mine_a, col,
    raw, rot_all, leaves, sent_leaf, diag, diag_part, diag_all,
    pair_part, got_p, mine_p, zs_p, pair_all, piece_p,
    cross_part, got_x, mine_x, zs_x, cross_all, piece_x,
    load_sem, start_sem, near, far, c_sem, y_sem, a_sem, b_sem, d_sem, raw_sem, rot_sem, leaf_sem, e_sem, g_sem, p_sem, x_sem,
):
    z, y, c, x = (lax.axis_index(name) for name in ("z", "y", "c", "x"))
    j = y * NC + c
    m = y * NZ + z
    t = x * ROW + j
    quarter = f.shape[0] // NX
    early = raw.shape[1]
    late = quarter - early
    pending = []

    def send(src, dst, sems, **where):
        pltpu.make_async_remote_copy(
            src_ref=src, dst_ref=dst, send_sem=sems.at[0], recv_sem=sems.at[1],
            device_id=where, device_id_type=MESH,
        ).start()

    def await_bytes(ref, sem):
        pltpu.make_async_copy(ref, ref, sem).wait()

    def arrived(ref, sems):
        pending.append((ref, sems.at[0]))
        await_bytes(ref, sems.at[1])

    def greet(**where):
        pl.semaphore_signal(pltpu.get_barrier_semaphore(), inc=1, device_id=where, device_id_type=MESH)

    def away(index, k, size):
        step = (k + 1) // 2
        return lax.rem(index + size // 2 + jnp.where(lax.rem(k, 2) == 1, size - step, step), size)

    def in_row(k):
        peer_y, peer_c = away(y, k // NC, NY), away(c, lax.rem(k, NC), NC)
        return peer_y * NC + peer_c, dict(y=peer_y, c=peer_c)

    def in_sheet(k):
        return dict(z=away(z, k // NY, NZ), y=away(y, lax.rem(k, NY), NY))

    def in_plane(k):
        peer_x = away(x, k // ROW, NX)
        peer, where = in_row(lax.rem(k, ROW))
        return peer_x * ROW + peer, dict(x=peer_x, **where)

    loads = []
    for k in range(NX):
        rows = pl.ds(k * quarter, quarter)
        loads.append(pltpu.make_async_copy(fields.at[rows], f.at[rows], load_sem.at[k]))
    own_early = pl.ds(pl.multiple_of(x * quarter, quarter), early)
    loads.append(pltpu.make_async_copy(fields.at[own_early], raw.at[x], load_sem.at[NX]))
    for k, (src, dst) in enumerate([(start_local, s_local), (start_pair, s_pair), (start_root, s_root)]):
        loads.append(pltpu.make_async_copy(src, dst, start_sem.at[k]))
    for load in loads:
        load.start()

    for k in range(NX - 1):
        greet(x=away(x, k, NX), c=0)
    for k in range(NY - 1):
        greet(y=away(y, k, NY), c=0)

    @pl.when(c == 1)
    def _():
        greet(c=0)

    @pl.loop(0, NZ - 1)
    def _(k):
        greet(z=away(z, k, NZ), c=1)

    total = None
    for k in range(NX):
        loads[k].wait()
        part = f[pl.ds(k * quarter, quarter)]
        term = product_t(part, part)
        total = term if total is None else total + term
    gram[...] = total

    @pl.when(c == 0)
    def _():
        pl.semaphore_wait(pltpu.get_barrier_semaphore(), NC * (NX - 1 + NY - 1) + 1)
        pl.semaphore_signal(near, inc=1, device_id=dict(c=1), device_id_type=MESH)

    @pl.when(c == 1)
    def _():
        pl.semaphore_wait(near, 1)

    half = gram.shape[0] // NC
    send(gram.at[pl.ds(pl.multiple_of((1 - c) * half, 8), half)], got_c, c_sem, c=1 - c)

    @pl.loop(0, early // PIECE)
    def _(k):
        for d in (2, 1, 3):
            peer = lax.rem(x + d, NX)
            rows = pl.ds(pl.multiple_of(peer * quarter + k * PIECE, PIECE), PIECE)
            send(f.at[rows], raw.at[x, pl.ds(pl.multiple_of(k * PIECE, PIECE), PIECE)], raw_sem, x=peer)

    arrived(got_c, c_sem)
    kept = gram[pl.ds(pl.multiple_of(c * half, 8), half)] + got_c[...]
    kept_y[...] = kept

    strip = half // NY
    for k in range(NY - 1):
        peer = away(y, k, NY)
        send(kept_y.at[pl.ds(pl.multiple_of(peer * strip, 8), strip)], got_y.at[k], y_sem, y=peer)
    arrived(got_y, y_sem)
    sums = kept_y[pl.ds(pl.multiple_of(y * strip, 8), strip)] + got_y[...].sum(axis=0)
    for n in range(NZ):
        r, s = 8 * (n // 2), 128 * (n % 2)
        part_a[n] = sums[r:r + 8, s:s + 128]

    @pl.when(c == 1)
    def _():
        pl.semaphore_wait(pltpu.get_barrier_semaphore(), NC * (NZ - 1))
        pl.semaphore_signal(far, inc=1, device_id=dict(c=0), device_id_type=MESH)

    @pl.when(c == 0)
    def _():
        pl.semaphore_wait(far, 1)

    @pl.loop(0, NZ - 1)
    def _(k):
        peer = away(z, k, NZ)
        send(part_a.at[peer], got_a.at[k], a_sem, z=peer)

    arrived(got_a, a_sem)
    tile = (part_a[z] + got_a[...].sum(axis=0)) * inverse_count
    mine_a[...] = tile
    col[c, m] = tile

    @pl.loop(0, SHEET - 1)
    def _(d):
        send(mine_a, col.at[c, m], b_sem, **in_sheet(d))

    arrived(col.at[0, pl.ds(0, SHEET - 1)], b_sem)
    send(col.at[c], col.at[c], d_sem, c=1 - c)
    arrived(col.at[0], d_sem)
    whole = jnp.concatenate(
        [
            jnp.concatenate([col[n, 2 * k], col[n, 2 * k + 1]], axis=1)
            for n in range(NC)
            for k in range(SHEET // 2)
        ],
        axis=0,
    )
    for load in loads[NX:]:
        load.wait()
    bases = [s_local[...].T]
    for _ in range(POWER):
        bases = power_steps([whole], bases)
    rotation = bases[0].T.astype(BF16)

    rot_all[x] = rotation
    for d in (2, 1, 3):
        send(rot_all.at[x], rot_all.at[x], rot_sem, x=lax.rem(x + d, NX))
    for n, d in enumerate((2, 1, 3)):
        peer = lax.rem(x + d, NX)
        rows = pl.ds(pl.multiple_of(peer * quarter + early, PIECE), late)
        sent_leaf[n] = product(f[rows], rotation).astype(BF16)
        send(sent_leaf.at[n], leaves.at[x, pl.ds(early, late)], leaf_sem, x=peer)

    diag[...] = turned(whole, rotation, rotation)
    part16 = pl.ds(pl.multiple_of(j * 16, 16), 16)
    diag_part[x] = diag[part16]
    for d in (1, 2, 3):
        send(diag.at[part16], diag_part.at[x], e_sem, x=lax.rem(x + d, NX))

    own_late = pl.ds(pl.multiple_of(x * quarter + early, PIECE), late)
    leaves[x, pl.ds(early, late)] = product(f[own_late], rotation).astype(BF16)

    arrived(raw.at[pl.ds(0, NX - 1)], raw_sem)
    arrived(rot_all.at[pl.ds(0, NX - 1)], rot_sem)
    for b in range(NX):
        leaves[b, pl.ds(0, early)] = product(raw[b], rot_all[b]).astype(BF16)
    arrived(leaves.at[pl.ds(0, NX - 1), pl.ds(early, late)], leaf_sem)

    pair_part[0:128] = product_t(leaves[0], leaves[1])
    pair_part[128:256] = product_t(leaves[2], leaves[3])

    @pl.loop(0, PLANE - 1)
    def _(d):
        peer, where = in_plane(d)
        send(pair_part.at[pl.ds(pl.multiple_of(peer * 8, 8), 8)], got_p.at[d], p_sem.at[0], **where)

    left = jnp.concatenate([leaves[0], leaves[1]], axis=1)
    right = jnp.concatenate([leaves[2], leaves[3]], axis=1)
    cross_part[...] = product_t(left, right)

    @pl.loop(0, PLANE - 1)
    def _(d):
        peer, where = in_plane(d)
        send(cross_part.at[pl.ds(pl.multiple_of(peer * 8, 8), 8)], got_x.at[d], x_sem.at[0], **where)

    arrived(diag_part.at[pl.ds(0, NX - 1)], e_sem)
    diag_all[j] = diag_part[...]

    @pl.loop(0, ROW - 1)
    def _(d):
        send(diag_part, diag_all.at[j], g_sem, **in_row(d)[1])

    my8 = pl.ds(pl.multiple_of(t * 8, 8), 8)

    def over_z(got, part, mine, zs, sems):
        arrived(got, sems.at[0])
        value = part[my8] + got[...].sum(axis=0)
        mine[...] = value
        zs[z] = value

        @pl.loop(0, NZ - 1)
        def _(d):
            send(mine, zs.at[z], sems.at[1], z=away(z, d, NZ))

    def to_plane(zs, piece, whole_ref, sems):
        arrived(zs.at[pl.ds(0, NZ - 1)], sems.at[1])
        value = zs[...].sum(axis=0) * inverse_count
        piece[...] = value
        whole_ref[my8] = value

        @pl.loop(0, PLANE - 1)
        def _(d):
            send(piece, whole_ref.at[my8], sems.at[2], **in_plane(d)[1])

    def from_plane(whole_ref, sems):
        arrived(whole_ref.at[pl.ds(0, 8 * (PLANE - 1))], sems.at[2])

    over_z(got_p, pair_part, mine_p, zs_p, p_sem)
    to_plane(zs_p, piece_p, pair_all, p_sem)
    over_z(got_x, cross_part, mine_x, zs_x, x_sem)
    arrived(diag_all.at[pl.ds(0, ROW - 1)], g_sem)
    diags = [jnp.concatenate([diag_all[n, b] for n in range(ROW)], axis=0) for b in range(NX)]
    from_plane(pair_all, p_sem)

    def pair_gram(n):
        block = pair_all[128 * n:128 * n + 128]
        top = jnp.concatenate([diags[2 * n], block], axis=1)
        low = jnp.concatenate([block.T, diags[2 * n + 1]], axis=1)
        return jnp.concatenate([top, low], axis=0)

    grams = [pair_gram(0), pair_gram(1)]
    bases = power_steps(grams, [s_pair[n].T for n in range(2)])
    to_plane(zs_x, piece_x, cross_all, x_sem)
    bases = power_steps(grams, bases)
    rotations = [basis.T.astype(BF16) for basis in bases]
    first = turned(grams[0], rotations[0], rotations[0])
    second = turned(grams[1], rotations[1], rotations[1])
    from_plane(cross_all, x_sem)
    mixed = turned(cross_all[...], rotations[0], rotations[1])
    root_gram = jnp.concatenate(
        [jnp.concatenate([first, mixed], axis=1), jnp.concatenate([mixed.T, second], axis=1)], axis=0
    )
    branch = jnp.concatenate(
        [product(left, rotations[0]).astype(BF16), product(right, rotations[1]).astype(BF16)], axis=1
    )
    bases = [s_root[...].T]
    for _ in range(POWER):
        bases = power_steps([root_gram], bases)
    out[...] = product(branch, bases[0].T.astype(BF16)).astype(BF16)

    for ref, sem in pending:
        await_bytes(ref, sem)


def on_device(points, fields, start_local, start_pair, start_root):
    rows, snaps = fields.shape
    vmem = pltpu.VMEM
    dma = pltpu.SemaphoreType.DMA
    quarter = rows // NX
    early = EARLY * quarter // 8
    scratch = [
        vmem((rows, snaps), BF16), vmem(start_local.shape, F32), vmem(start_pair.shape, F32), vmem(start_root.shape, F32),
        vmem((snaps, snaps), F32), vmem((snaps // NC, snaps), F32), vmem((snaps // NC, snaps), F32),
        vmem((NY - 1, snaps // NC // NY, snaps), F32), vmem((NZ, 8, 128), F32), vmem((NZ - 1, 8, 128), F32), vmem((8, 128), F32), vmem((NC, SHEET, 8, 128), F32),
        vmem((NX, early, snaps), BF16), vmem((NX, snaps, RANK), BF16),
        vmem((NX, quarter, RANK), BF16), vmem((NX - 1, quarter - early, RANK), BF16), vmem((RANK, RANK), F32),
        vmem((NX, 16, RANK), F32), vmem((ROW, NX, 16, RANK), F32),
        vmem((256, 128), F32), vmem((PLANE - 1, 8, 128), F32), vmem((8, 128), F32), vmem((NZ, 8, 128), F32),
        vmem((256, 128), F32), vmem((8, 128), F32),
        vmem((256, 256), F32), vmem((PLANE - 1, 8, 256), F32), vmem((8, 256), F32), vmem((NZ, 8, 256), F32),
        vmem((256, 256), F32), vmem((8, 256), F32),
        dma((NX + 1,)), dma((3,)), *[pltpu.SemaphoreType.REGULAR] * 2, *[dma((2,))] * 10, dma((3, 2)), dma((3, 2)),
    ]
    anywhere = pl.BlockSpec(memory_space=pltpu.HBM)
    return pl.pallas_call(
        functools.partial(body, 1.0 / points),
        out_shape=jax.ShapeDtypeStruct((quarter, RANK), BF16),
        in_specs=[anywhere] * 4,
        out_specs=pl.BlockSpec(memory_space=pltpu.VMEM),
        scratch_shapes=scratch,
        compiler_params=pltpu.CompilerParams(
            collective_id=0, has_side_effects=True, vmem_limit_bytes=48 * 2**20
        ),
        name="snapshot_modes",
    )(*(pltpu.with_memory_space_constraint(a, pltpu.HBM) for a in (fields, start_local, start_pair, start_root)))


def solution(mesh):
    split = Mesh(mesh.devices.reshape(NZ, NY, NC, mesh.shape["snap"]), ("z", "y", "c", "x"))
    grid = ("z", "y", "c")

    def whole(fields, start_local, start_pair, start_root):
        return jax.shard_map(
            functools.partial(on_device, fields.shape[0]),
            mesh=split,
            in_specs=(P(grid, "x"), P("x", None), P(), P()),
            out_specs=P((*grid, "x"), None),
            check_vma=False,
        )(fields, start_local, start_pair, start_root)

    return whole
```

```python
import functools

import jax
import jax.numpy as jnp
from jax import lax
from jax.experimental import pallas as pl
from jax.experimental.pallas import tpu as pltpu
from jax.sharding import Mesh
from jax.sharding import PartitionSpec as P

POWER = 2
NEWTON = 8
RANK = 128
NZ, NY, NC, NX = 8, 4, 2, 4
ROW = NY * NC
SHEET = NZ * NY
PLANE = NX * ROW
EARLY = 5
PIECE = 192
MESH = pl.DeviceIdType.MESH
F32 = jnp.float32
BF16 = jnp.bfloat16


def product(a, b):
    return jnp.dot(a, b, preferred_element_type=F32)


def product_t(a, b):
    return lax.dot_general(a, b, (((0,), (0,)), ((), ())), preferred_element_type=F32)


def halves(a):
    high = a.astype(BF16)
    return high, (a - high.astype(F32)).astype(BF16)


def three_products(a, b, dims):
    (a_high, a_low), (b_high, b_low) = halves(a), halves(b)
    (a_dim,), (b_dim,) = dims
    left = jnp.concatenate([a_high, a_high, a_low], axis=a_dim)
    right = jnp.concatenate([b_high, b_low, b_high], axis=b_dim)
    return lax.dot_general(left, right, (dims, ((), ())), preferred_element_type=F32)


def power_steps(grams, bases):
    steps = [three_products(basis, gram, ((1,), (0,))) for gram, basis in zip(grams, bases)]
    flat = [w * (1.0 / jnp.sqrt(jnp.sum(w * w) + 1e-06)) for w in steps]
    for _ in range(NEWTON):
        inner = [three_products(w, w, ((1,), (1,))) for w in flat]
        flat = [1.5 * w - 0.5 * three_products(s, w, ((1,), (0,))) for s, w in zip(inner, flat)]
    return flat


def turned(gram, left, right):
    high, low = halves(gram)
    middle = product(jnp.concatenate([high, low], axis=1), jnp.concatenate([right, right], axis=0))
    high, low = halves(middle)
    return product_t(jnp.concatenate([left, left], axis=0), jnp.concatenate([high, low], axis=0))


def body(
    inverse_count,
    fields, start_local, start_pair, start_root,
    out,
    f, s_local, s_pair, s_root,
    gram, got_c, kept_y, got_y, part_a, got_a, mine_a, col,
    raw, rot_all, leaves, sent_leaf, diag, diag_part, diag_all,
    pair_part, got_p, mine_p, zs_p, pair_all, piece_p,
    cross_part, got_x, mine_x, zs_x, cross_all, piece_x,
    load_sem, start_sem, near, far, c_sem, y_sem, a_sem, b_sem, d_sem, raw_sem, rot_sem, leaf_sem, e_sem, g_sem, p_sem, x_sem,
):
    z, y, c, x = (lax.axis_index(name) for name in ("z", "y", "c", "x"))
    j = y * NC + c
    m = y * NZ + z
    t = x * ROW + j
    quarter = f.shape[0] // NX
    early = raw.shape[1]
    late = quarter - early
    pending = []

    def send(src, dst, sems, **where):
        pltpu.make_async_remote_copy(
            src_ref=src, dst_ref=dst, send_sem=sems.at[0], recv_sem=sems.at[1],
            device_id=where, device_id_type=MESH,
        ).start()

    def await_bytes(ref, sem):
        pltpu.make_async_copy(ref, ref, sem).wait()

    def arrived(ref, sems):
        pending.append((ref, sems.at[0]))
        await_bytes(ref, sems.at[1])

    def greet(**where):
        pl.semaphore_signal(pltpu.get_barrier_semaphore(), inc=1, device_id=where, device_id_type=MESH)

    def away(index, k, size):
        step = (k + 1) // 2
        return lax.rem(index + size // 2 + jnp.where(lax.rem(k, 2) == 1, size - step, step), size)

    def in_row(k):
        peer_y, peer_c = away(y, k // NC, NY), away(c, lax.rem(k, NC), NC)
        return peer_y * NC + peer_c, dict(y=peer_y, c=peer_c)

    def in_sheet(k):
        return dict(z=away(z, k // NY, NZ), y=away(y, lax.rem(k, NY), NY))

    def in_plane(k):
        peer_x = away(x, k // ROW, NX)
        peer, where = in_row(lax.rem(k, ROW))
        return peer_x * ROW + peer, dict(x=peer_x, **where)

    loads = []
    for k in range(NX):
        rows = pl.ds(k * quarter, quarter)
        loads.append(pltpu.make_async_copy(fields.at[rows], f.at[rows], load_sem.at[k]))
    own_early = pl.ds(pl.multiple_of(x * quarter, quarter), early)
    loads.append(pltpu.make_async_copy(fields.at[own_early], raw.at[x], load_sem.at[NX]))
    for k, (src, dst) in enumerate([(start_local, s_local), (start_pair, s_pair), (start_root, s_root)]):
        loads.append(pltpu.make_async_copy(src, dst, start_sem.at[k]))
    for load in loads:
        load.start()

    for k in range(NX - 1):
        greet(x=away(x, k, NX), c=0)
    for k in range(NY - 1):
        greet(y=away(y, k, NY), c=0)

    @pl.when(c == 1)
    def _():
        greet(c=0)

    @pl.loop(0, NZ - 1)
    def _(k):
        greet(z=away(z, k, NZ), c=1)

    total = None
    for k in range(NX):
        loads[k].wait()
        part = f[pl.ds(k * quarter, quarter)]
        term = product_t(part, part)
        total = term if total is None else total + term
    gram[...] = total

    @pl.when(c == 0)
    def _():
        pl.semaphore_wait(pltpu.get_barrier_semaphore(), NC * (NX - 1 + NY - 1) + 1)
        pl.semaphore_signal(near, inc=1, device_id=dict(c=1), device_id_type=MESH)

    @pl.when(c == 1)
    def _():
        pl.semaphore_wait(near, 1)

    half = gram.shape[0] // NC
    send(gram.at[pl.ds(pl.multiple_of((1 - c) * half, 8), half)], got_c, c_sem, c=1 - c)

    @pl.loop(0, early // PIECE)
    def _(k):
        for d in (2, 1, 3):
            peer = lax.rem(x + d, NX)
            rows = pl.ds(pl.multiple_of(peer * quarter + k * PIECE, PIECE), PIECE)
            send(f.at[rows], raw.at[x, pl.ds(pl.multiple_of(k * PIECE, PIECE), PIECE)], raw_sem, x=peer)

    arrived(got_c, c_sem)
    kept = gram[pl.ds(pl.multiple_of(c * half, 8), half)] + got_c[...]
    kept_y[...] = kept

    strip = half // NY
    for k in range(NY - 1):
        peer = away(y, k, NY)
        send(kept_y.at[pl.ds(pl.multiple_of(peer * strip, 8), strip)], got_y.at[k], y_sem, y=peer)
    arrived(got_y, y_sem)
    sums = kept_y[pl.ds(pl.multiple_of(y * strip, 8), strip)] + got_y[...].sum(axis=0)
    for n in range(NZ):
        r, s = 8 * (n // 2), 128 * (n % 2)
        part_a[n] = sums[r:r + 8, s:s + 128]

    @pl.when(c == 1)
    def _():
        pl.semaphore_wait(pltpu.get_barrier_semaphore(), NC * (NZ - 1))
        pl.semaphore_signal(far, inc=1, device_id=dict(c=0), device_id_type=MESH)

    @pl.when(c == 0)
    def _():
        pl.semaphore_wait(far, 1)

    @pl.loop(0, NZ - 1)
    def _(k):
        peer = away(z, k, NZ)
        send(part_a.at[peer], got_a.at[k], a_sem, z=peer)

    arrived(got_a, a_sem)
    tile = (part_a[z] + got_a[...].sum(axis=0)) * inverse_count
    mine_a[...] = tile
    col[c, m] = tile

    @pl.loop(0, SHEET - 1)
    def _(d):
        send(mine_a, col.at[c, m], b_sem, **in_sheet(d))

    arrived(col.at[0, pl.ds(0, SHEET - 1)], b_sem)
    send(col.at[c], col.at[c], d_sem, c=1 - c)
    arrived(col.at[0], d_sem)
    whole = jnp.concatenate(
        [
            jnp.concatenate([col[n, 2 * k], col[n, 2 * k + 1]], axis=1)
            for n in range(NC)
            for k in range(SHEET // 2)
        ],
        axis=0,
    )
    for load in loads[NX:]:
        load.wait()
    bases = [s_local[...].T]
    for _ in range(POWER):
        bases = power_steps([whole], bases)
    rotation = bases[0].T.astype(BF16)

    rot_all[x] = rotation
    for d in (2, 1, 3):
        send(rot_all.at[x], rot_all.at[x], rot_sem, x=lax.rem(x + d, NX))
    for n, d in enumerate((2, 1, 3)):
        peer = lax.rem(x + d, NX)
        rows = pl.ds(pl.multiple_of(peer * quarter + early, PIECE), late)
        sent_leaf[n] = product(f[rows], rotation).astype(BF16)
        send(sent_leaf.at[n], leaves.at[x, pl.ds(early, late)], leaf_sem, x=peer)

    diag[...] = turned(whole, rotation, rotation)
    part16 = pl.ds(pl.multiple_of(j * 16, 16), 16)
    diag_part[x] = diag[part16]
    for d in (1, 2, 3):
        send(diag.at[part16], diag_part.at[x], e_sem, x=lax.rem(x + d, NX))

    own_late = pl.ds(pl.multiple_of(x * quarter + early, PIECE), late)
    leaves[x, pl.ds(early, late)] = product(f[own_late], rotation).astype(BF16)

    leaves[x, pl.ds(0, early)] = product(raw[x], rotation).astype(BF16)
    arrived(raw.at[pl.ds(0, NX - 1)], raw_sem)
    arrived(rot_all.at[pl.ds(0, NX - 1)], rot_sem)
    for d in (1, 2, 3):
        b = lax.rem(x + d, NX)
        leaves[b, pl.ds(0, early)] = product(raw[b], rot_all[b]).astype(BF16)

    def joined(n, rows):
        return jnp.concatenate([leaves[2 * n, rows], leaves[2 * n + 1, rows]], axis=1)

    first_rows, last_rows, all_rows = slice(0, early), slice(early, quarter), slice(0, quarter)
    for n in range(2):
        pair_part[128 * n:128 * n + 128] = product_t(leaves[2 * n, first_rows], leaves[2 * n + 1, first_rows])
    arrived(leaves.at[pl.ds(0, NX - 1), pl.ds(early, late)], leaf_sem)
    for n in range(2):
        pair_part[128 * n:128 * n + 128] += product_t(leaves[2 * n, last_rows], leaves[2 * n + 1, last_rows])

    @pl.loop(0, PLANE - 1)
    def _(d):
        peer, where = in_plane(d)
        send(pair_part.at[pl.ds(pl.multiple_of(peer * 8, 8), 8)], got_p.at[d], p_sem.at[0], **where)

    cross_part[...] = product_t(joined(0, all_rows), joined(1, all_rows))

    @pl.loop(0, PLANE - 1)
    def _(d):
        peer, where = in_plane(d)
        send(cross_part.at[pl.ds(pl.multiple_of(peer * 8, 8), 8)], got_x.at[d], x_sem.at[0], **where)

    arrived(diag_part.at[pl.ds(0, NX - 1)], e_sem)
    diag_all[j] = diag_part[...]

    @pl.loop(0, ROW - 1)
    def _(d):
        send(diag_part, diag_all.at[j], g_sem, **in_row(d)[1])

    my8 = pl.ds(pl.multiple_of(t * 8, 8), 8)

    def over_z(got, part, mine, zs, sems):
        arrived(got, sems.at[0])
        value = part[my8] + got[...].sum(axis=0)
        mine[...] = value
        zs[z] = value

        @pl.loop(0, NZ - 1)
        def _(d):
            send(mine, zs.at[z], sems.at[1], z=away(z, d, NZ))

    def to_plane(zs, piece, whole_ref, sems):
        arrived(zs.at[pl.ds(0, NZ - 1)], sems.at[1])
        value = zs[...].sum(axis=0) * inverse_count
        piece[...] = value
        whole_ref[my8] = value

        @pl.loop(0, PLANE - 1)
        def _(d):
            send(piece, whole_ref.at[my8], sems.at[2], **in_plane(d)[1])

    def from_plane(whole_ref, sems):
        arrived(whole_ref.at[pl.ds(0, 8 * (PLANE - 1))], sems.at[2])

    over_z(got_p, pair_part, mine_p, zs_p, p_sem)
    to_plane(zs_p, piece_p, pair_all, p_sem)
    over_z(got_x, cross_part, mine_x, zs_x, x_sem)
    arrived(diag_all.at[pl.ds(0, ROW - 1)], g_sem)
    diags = [jnp.concatenate([diag_all[n, b] for n in range(ROW)], axis=0) for b in range(NX)]
    from_plane(pair_all, p_sem)

    def pair_gram(n):
        block = pair_all[128 * n:128 * n + 128]
        top = jnp.concatenate([diags[2 * n], block], axis=1)
        low = jnp.concatenate([block.T, diags[2 * n + 1]], axis=1)
        return jnp.concatenate([top, low], axis=0)

    grams = [pair_gram(0), pair_gram(1)]
    bases = power_steps(grams, [s_pair[n].T for n in range(2)])
    to_plane(zs_x, piece_x, cross_all, x_sem)
    bases = power_steps(grams, bases)
    rotations = [basis.T.astype(BF16) for basis in bases]
    first = turned(grams[0], rotations[0], rotations[0])
    second = turned(grams[1], rotations[1], rotations[1])
    from_plane(cross_all, x_sem)
    mixed = turned(cross_all[...], rotations[0], rotations[1])
    root_gram = jnp.concatenate(
        [jnp.concatenate([first, mixed], axis=1), jnp.concatenate([mixed.T, second], axis=1)], axis=0
    )
    branch = jnp.concatenate(
        [product(joined(n, all_rows), rotations[n]).astype(BF16) for n in range(2)], axis=1
    )
    bases = [s_root[...].T]
    for _ in range(POWER):
        bases = power_steps([root_gram], bases)
    out[...] = product(branch, bases[0].T.astype(BF16)).astype(BF16)

    for ref, sem in pending:
        await_bytes(ref, sem)


def on_device(points, fields, start_local, start_pair, start_root):
    rows, snaps = fields.shape
    vmem = pltpu.VMEM
    dma = pltpu.SemaphoreType.DMA
    quarter = rows // NX
    early = EARLY * quarter // 8
    scratch = [
        vmem((rows, snaps), BF16), vmem(start_local.shape, F32), vmem(start_pair.shape, F32), vmem(start_root.shape, F32),
        vmem((snaps, snaps), F32), vmem((snaps // NC, snaps), F32), vmem((snaps // NC, snaps), F32),
        vmem((NY - 1, snaps // NC // NY, snaps), F32), vmem((NZ, 8, 128), F32), vmem((NZ - 1, 8, 128), F32), vmem((8, 128), F32), vmem((NC, SHEET, 8, 128), F32),
        vmem((NX, early, snaps), BF16), vmem((NX, snaps, RANK), BF16),
        vmem((NX, quarter, RANK), BF16), vmem((NX - 1, quarter - early, RANK), BF16), vmem((RANK, RANK), F32),
        vmem((NX, 16, RANK), F32), vmem((ROW, NX, 16, RANK), F32),
        vmem((256, 128), F32), vmem((PLANE - 1, 8, 128), F32), vmem((8, 128), F32), vmem((NZ, 8, 128), F32),
        vmem((256, 128), F32), vmem((8, 128), F32),
        vmem((256, 256), F32), vmem((PLANE - 1, 8, 256), F32), vmem((8, 256), F32), vmem((NZ, 8, 256), F32),
        vmem((256, 256), F32), vmem((8, 256), F32),
        dma((NX + 1,)), dma((3,)), *[pltpu.SemaphoreType.REGULAR] * 2, *[dma((2,))] * 10, dma((3, 2)), dma((3, 2)),
    ]
    anywhere = pl.BlockSpec(memory_space=pltpu.HBM)
    return pl.pallas_call(
        functools.partial(body, 1.0 / points),
        out_shape=jax.ShapeDtypeStruct((quarter, RANK), BF16),
        in_specs=[anywhere] * 4,
        out_specs=pl.BlockSpec(memory_space=pltpu.VMEM),
        scratch_shapes=scratch,
        compiler_params=pltpu.CompilerParams(
            collective_id=0, has_side_effects=True, vmem_limit_bytes=48 * 2**20
        ),
        name="snapshot_modes",
    )(*(pltpu.with_memory_space_constraint(a, pltpu.HBM) for a in (fields, start_local, start_pair, start_root)))


def solution(mesh):
    split = Mesh(mesh.devices.reshape(NZ, NY, NC, mesh.shape["snap"]), ("z", "y", "c", "x"))
    grid = ("z", "y", "c")

    def whole(fields, start_local, start_pair, start_root):
        return jax.shard_map(
            functools.partial(on_device, fields.shape[0]),
            mesh=split,
            in_specs=(P(grid, "x"), P("x", None), P(), P()),
            out_specs=P((*grid, "x"), None),
            check_vma=False,
        )(fields, start_local, start_pair, start_root)

    return whole
```

```python
import functools

import jax
import jax.numpy as jnp
from jax import lax
from jax.experimental import pallas as pl
from jax.experimental.pallas import tpu as pltpu
from jax.sharding import Mesh
from jax.sharding import PartitionSpec as P

POWER = 2
NEWTON = 8
RANK = 128
NZ, NY, NC, NX = 8, 4, 2, 4
ROW = NY * NC
SHEET = NZ * NY
PLANE = NX * ROW
EARLY = 5
PIECE = 192
MESH = pl.DeviceIdType.MESH
F32 = jnp.float32
BF16 = jnp.bfloat16


def product(a, b):
    return jnp.dot(a, b, preferred_element_type=F32)


def product_t(a, b):
    return lax.dot_general(a, b, (((0,), (0,)), ((), ())), preferred_element_type=F32)


def halves(a):
    high = a.astype(BF16)
    return high, (a - high.astype(F32)).astype(BF16)


def three_products(a, b, dims):
    (a_high, a_low), (b_high, b_low) = halves(a), halves(b)
    (a_dim,), (b_dim,) = dims
    left = jnp.concatenate([a_high, a_high, a_low], axis=a_dim)
    right = jnp.concatenate([b_high, b_low, b_high], axis=b_dim)
    return lax.dot_general(left, right, (dims, ((), ())), preferred_element_type=F32)


def power_steps(grams, bases):
    steps = [three_products(basis, gram, ((1,), (0,))) for gram, basis in zip(grams, bases)]
    flat = [w * (1.0 / jnp.sqrt(jnp.sum(w * w) + 1e-06)) for w in steps]
    for _ in range(NEWTON):
        inner = [three_products(w, w, ((1,), (1,))) for w in flat]
        flat = [1.5 * w - 0.5 * three_products(s, w, ((1,), (0,))) for s, w in zip(inner, flat)]
    return flat


def turned(gram, left, right):
    high, low = halves(gram)
    middle = product(jnp.concatenate([high, low], axis=1), jnp.concatenate([right, right], axis=0))
    high, low = halves(middle)
    return product_t(jnp.concatenate([left, left], axis=0), jnp.concatenate([high, low], axis=0))


def body(
    inverse_count,
    fields, start_local, start_pair, start_root,
    out,
    f, s_local, s_pair, s_root,
    gram, got_c, kept_y, got_y, part_a, got_a, mine_a, col,
    raw, rot_all, leaves, sent_leaf, diag, diag_part, diag_all,
    pair_part, got_p, mine_p, zs_p, pair_all, piece_p,
    cross_part, got_x, mine_x, zs_x, cross_all, piece_x,
    load_sem, start_sem, near, far, c_sem, y_sem, a_sem, b_sem, d_sem, raw_sem, rot_sem, leaf_sem, e_sem, g_sem, p_sem, x_sem,
):
    z, y, c, x = (lax.axis_index(name) for name in ("z", "y", "c", "x"))
    j = y * NC + c
    m = y * NZ + z
    t = x * ROW + j
    quarter = f.shape[0] // NX
    early = raw.shape[1]
    late = quarter - early
    pending = []

    def send(src, dst, sems, **where):
        pltpu.make_async_remote_copy(
            src_ref=src, dst_ref=dst, send_sem=sems.at[0], recv_sem=sems.at[1],
            device_id=where, device_id_type=MESH,
        ).start()

    def await_bytes(ref, sem):
        pltpu.make_async_copy(ref, ref, sem).wait()

    def arrived(ref, sems):
        pending.append((ref, sems.at[0]))
        await_bytes(ref, sems.at[1])

    def greet(**where):
        pl.semaphore_signal(pltpu.get_barrier_semaphore(), inc=1, device_id=where, device_id_type=MESH)

    def away(index, k, size):
        step = (k + 1) // 2
        return lax.rem(index + size // 2 + jnp.where(lax.rem(k, 2) == 1, size - step, step), size)

    def in_row(k):
        peer_y, peer_c = away(y, k // NC, NY), away(c, lax.rem(k, NC), NC)
        return peer_y * NC + peer_c, dict(y=peer_y, c=peer_c)

    def in_sheet(k):
        return dict(z=away(z, k // NY, NZ), y=away(y, lax.rem(k, NY), NY))

    def in_plane(k):
        peer_x = away(x, k // ROW, NX)
        peer, where = in_row(lax.rem(k, ROW))
        return peer_x * ROW + peer, dict(x=peer_x, **where)

    loads = []
    for k in range(NX):
        rows = pl.ds(k * quarter, quarter)
        loads.append(pltpu.make_async_copy(fields.at[rows], f.at[rows], load_sem.at[k]))
    own_early = pl.ds(pl.multiple_of(x * quarter, quarter), early)
    loads.append(pltpu.make_async_copy(fields.at[own_early], raw.at[x], load_sem.at[NX]))
    for k, (src, dst) in enumerate([(start_local, s_local), (start_pair, s_pair), (start_root, s_root)]):
        loads.append(pltpu.make_async_copy(src, dst, start_sem.at[k]))
    for load in loads:
        load.start()

    for k in range(NX - 1):
        greet(x=away(x, k, NX), c=0)
    for k in range(NY - 1):
        greet(y=away(y, k, NY), c=0)

    @pl.when(c == 1)
    def _():
        greet(c=0)

    @pl.loop(0, NZ - 1)
    def _(k):
        greet(z=away(z, k, NZ), c=1)

    total = None
    for k in range(NX):
        loads[k].wait()
        part = f[pl.ds(k * quarter, quarter)]
        term = product_t(part, part)
        total = term if total is None else total + term
    gram[...] = total

    @pl.when(c == 0)
    def _():
        pl.semaphore_wait(pltpu.get_barrier_semaphore(), NC * (NX - 1 + NY - 1) + 1)
        pl.semaphore_signal(near, inc=1, device_id=dict(c=1), device_id_type=MESH)

    @pl.when(c == 1)
    def _():
        pl.semaphore_wait(near, 1)

    half = gram.shape[0] // NC
    send(gram.at[pl.ds(pl.multiple_of((1 - c) * half, 8), half)], got_c, c_sem, c=1 - c)

    @pl.loop(0, early // PIECE)
    def _(k):
        for d in (2, 1, 3):
            peer = lax.rem(x + d, NX)
            rows = pl.ds(pl.multiple_of(peer * quarter + k * PIECE, PIECE), PIECE)
            send(f.at[rows], raw.at[x, pl.ds(pl.multiple_of(k * PIECE, PIECE), PIECE)], raw_sem, x=peer)

    arrived(got_c, c_sem)
    kept = gram[pl.ds(pl.multiple_of(c * half, 8), half)] + got_c[...]
    kept_y[...] = kept

    strip = half // NY
    for k in range(NY - 1):
        peer = away(y, k, NY)
        send(kept_y.at[pl.ds(pl.multiple_of(peer * strip, 8), strip)], got_y.at[k], y_sem, y=peer)
    arrived(got_y, y_sem)
    sums = kept_y[pl.ds(pl.multiple_of(y * strip, 8), strip)] + got_y[...].sum(axis=0)
    for n in range(NZ):
        r, s = 8 * (n // 2), 128 * (n % 2)
        part_a[n] = sums[r:r + 8, s:s + 128]

    @pl.when(c == 1)
    def _():
        pl.semaphore_wait(pltpu.get_barrier_semaphore(), NC * (NZ - 1))
        pl.semaphore_signal(far, inc=1, device_id=dict(c=0), device_id_type=MESH)

    @pl.when(c == 0)
    def _():
        pl.semaphore_wait(far, 1)

    @pl.loop(0, NZ - 1)
    def _(k):
        peer = away(z, k, NZ)
        send(part_a.at[peer], got_a.at[k], a_sem, z=peer)

    arrived(got_a, a_sem)
    tile = (part_a[z] + got_a[...].sum(axis=0)) * inverse_count
    mine_a[...] = tile
    col[c, m] = tile

    @pl.loop(0, SHEET - 1)
    def _(d):
        send(mine_a, col.at[c, m], b_sem, **in_sheet(d))

    arrived(col.at[0, pl.ds(0, SHEET - 1)], b_sem)
    send(col.at[c], col.at[c], d_sem, c=1 - c)
    arrived(col.at[0], d_sem)
    whole = jnp.concatenate(
        [
            jnp.concatenate([col[n, 2 * k], col[n, 2 * k + 1]], axis=1)
            for n in range(NC)
            for k in range(SHEET // 2)
        ],
        axis=0,
    )
    for load in loads[NX:]:
        load.wait()
    bases = [s_local[...].T]
    for _ in range(POWER):
        bases = power_steps([whole], bases)
    rotation = bases[0].T.astype(BF16)

    rot_all[x] = rotation
    for d in (2, 1, 3):
        send(rot_all.at[x], rot_all.at[x], rot_sem, x=lax.rem(x + d, NX))
    for n, d in enumerate((2, 1, 3)):
        peer = lax.rem(x + d, NX)
        rows = pl.ds(pl.multiple_of(peer * quarter + early, PIECE), late)
        sent_leaf[n] = product(f[rows], rotation).astype(BF16)
        send(sent_leaf.at[n], leaves.at[x, pl.ds(early, late)], leaf_sem, x=peer)

    diag[...] = turned(whole, rotation, rotation)
    part16 = pl.ds(pl.multiple_of(j * 16, 16), 16)
    diag_part[x] = diag[part16]
    for d in (1, 2, 3):
        send(diag.at[part16], diag_part.at[x], e_sem, x=lax.rem(x + d, NX))

    own_late = pl.ds(pl.multiple_of(x * quarter + early, PIECE), late)
    leaves[x, pl.ds(early, late)] = product(f[own_late], rotation).astype(BF16)

    leaves[x, pl.ds(0, early)] = product(raw[x], rotation).astype(BF16)
    arrived(raw.at[pl.ds(0, NX - 1)], raw_sem)
    arrived(rot_all.at[pl.ds(0, NX - 1)], rot_sem)
    for d in (1, 2, 3):
        b = lax.rem(x + d, NX)
        leaves[b, pl.ds(0, early)] = product(raw[b], rot_all[b]).astype(BF16)

    def joined(n, rows):
        return jnp.concatenate([leaves[2 * n, rows], leaves[2 * n + 1, rows]], axis=1)

    first_rows, last_rows, all_rows = slice(0, early), slice(early, quarter), slice(0, quarter)
    for n in range(2):
        pair_part[128 * n:128 * n + 128] = product_t(leaves[2 * n, first_rows], leaves[2 * n + 1, first_rows])
    arrived(leaves.at[pl.ds(0, NX - 1), pl.ds(early, late)], leaf_sem)
    for n in range(2):
        pair_part[128 * n:128 * n + 128] += product_t(leaves[2 * n, last_rows], leaves[2 * n + 1, last_rows])

    @pl.loop(0, PLANE - 1)
    def _(d):
        peer, where = in_plane(d)
        send(pair_part.at[pl.ds(pl.multiple_of(peer * 8, 8), 8)], got_p.at[d], p_sem.at[0], **where)

    cross_part[...] = product_t(joined(0, all_rows), joined(1, all_rows))

    @pl.loop(0, PLANE - 1)
    def _(d):
        peer, where = in_plane(d)
        send(cross_part.at[pl.ds(pl.multiple_of(peer * 8, 8), 8)], got_x.at[d], x_sem.at[0], **where)

    arrived(diag_part.at[pl.ds(0, NX - 1)], e_sem)
    diag_all[j] = diag_part[...]

    @pl.loop(0, ROW - 1)
    def _(d):
        send(diag_part, diag_all.at[j], g_sem, **in_row(d)[1])

    my8 = pl.ds(pl.multiple_of(t * 8, 8), 8)

    def over_z(got, part, mine, zs, sems):
        arrived(got, sems.at[0])
        value = part[my8] + got[...].sum(axis=0)
        mine[...] = value
        zs[z] = value

        @pl.loop(0, NZ - 1)
        def _(d):
            send(mine, zs.at[z], sems.at[1], z=away(z, d, NZ))

    def to_plane(zs, piece, whole_ref, sems):
        arrived(zs.at[pl.ds(0, NZ - 1)], sems.at[1])
        value = zs[...].sum(axis=0) * inverse_count
        piece[...] = value
        whole_ref[my8] = value

        @pl.loop(0, PLANE - 1)
        def _(d):
            send(piece, whole_ref.at[my8], sems.at[2], **in_plane(d)[1])

    def from_plane(whole_ref, sems):
        arrived(whole_ref.at[pl.ds(0, 8 * (PLANE - 1))], sems.at[2])

    over_z(got_p, pair_part, mine_p, zs_p, p_sem)
    over_z(got_x, cross_part, mine_x, zs_x, x_sem)
    to_plane(zs_p, piece_p, pair_all, p_sem)
    to_plane(zs_x, piece_x, cross_all, x_sem)
    arrived(diag_all.at[pl.ds(0, ROW - 1)], g_sem)
    diags = [jnp.concatenate([diag_all[n, b] for n in range(ROW)], axis=0) for b in range(NX)]
    from_plane(pair_all, p_sem)

    def pair_gram(n):
        block = pair_all[128 * n:128 * n + 128]
        top = jnp.concatenate([diags[2 * n], block], axis=1)
        low = jnp.concatenate([block.T, diags[2 * n + 1]], axis=1)
        return jnp.concatenate([top, low], axis=0)

    grams = [pair_gram(0), pair_gram(1)]
    bases = power_steps(grams, [s_pair[n].T for n in range(2)])
    bases = power_steps(grams, bases)
    rotations = [basis.T.astype(BF16) for basis in bases]
    first = turned(grams[0], rotations[0], rotations[0])
    second = turned(grams[1], rotations[1], rotations[1])
    from_plane(cross_all, x_sem)
    mixed = turned(cross_all[...], rotations[0], rotations[1])
    root_gram = jnp.concatenate(
        [jnp.concatenate([first, mixed], axis=1), jnp.concatenate([mixed.T, second], axis=1)], axis=0
    )
    branch = jnp.concatenate(
        [product(joined(n, all_rows), rotations[n]).astype(BF16) for n in range(2)], axis=1
    )
    bases = [s_root[...].T]
    for _ in range(POWER):
        bases = power_steps([root_gram], bases)
    out[...] = product(branch, bases[0].T.astype(BF16)).astype(BF16)

    for ref, sem in pending:
        await_bytes(ref, sem)


def on_device(points, fields, start_local, start_pair, start_root):
    rows, snaps = fields.shape
    vmem = pltpu.VMEM
    dma = pltpu.SemaphoreType.DMA
    quarter = rows // NX
    early = EARLY * quarter // 8
    scratch = [
        vmem((rows, snaps), BF16), vmem(start_local.shape, F32), vmem(start_pair.shape, F32), vmem(start_root.shape, F32),
        vmem((snaps, snaps), F32), vmem((snaps // NC, snaps), F32), vmem((snaps // NC, snaps), F32),
        vmem((NY - 1, snaps // NC // NY, snaps), F32), vmem((NZ, 8, 128), F32), vmem((NZ - 1, 8, 128), F32), vmem((8, 128), F32), vmem((NC, SHEET, 8, 128), F32),
        vmem((NX, early, snaps), BF16), vmem((NX, snaps, RANK), BF16),
        vmem((NX, quarter, RANK), BF16), vmem((NX - 1, quarter - early, RANK), BF16), vmem((RANK, RANK), F32),
        vmem((NX, 16, RANK), F32), vmem((ROW, NX, 16, RANK), F32),
        vmem((256, 128), F32), vmem((PLANE - 1, 8, 128), F32), vmem((8, 128), F32), vmem((NZ, 8, 128), F32),
        vmem((256, 128), F32), vmem((8, 128), F32),
        vmem((256, 256), F32), vmem((PLANE - 1, 8, 256), F32), vmem((8, 256), F32), vmem((NZ, 8, 256), F32),
        vmem((256, 256), F32), vmem((8, 256), F32),
        dma((NX + 1,)), dma((3,)), *[pltpu.SemaphoreType.REGULAR] * 2, *[dma((2,))] * 10, dma((3, 2)), dma((3, 2)),
    ]
    anywhere = pl.BlockSpec(memory_space=pltpu.HBM)
    return pl.pallas_call(
        functools.partial(body, 1.0 / points),
        out_shape=jax.ShapeDtypeStruct((quarter, RANK), BF16),
        in_specs=[anywhere] * 4,
        out_specs=pl.BlockSpec(memory_space=pltpu.VMEM),
        scratch_shapes=scratch,
        compiler_params=pltpu.CompilerParams(
            collective_id=0, has_side_effects=True, vmem_limit_bytes=48 * 2**20
        ),
        name="snapshot_modes",
    )(*(pltpu.with_memory_space_constraint(a, pltpu.HBM) for a in (fields, start_local, start_pair, start_root)))


def solution(mesh):
    split = Mesh(mesh.devices.reshape(NZ, NY, NC, mesh.shape["snap"]), ("z", "y", "c", "x"))
    grid = ("z", "y", "c")

    def whole(fields, start_local, start_pair, start_root):
        return jax.shard_map(
            functools.partial(on_device, fields.shape[0]),
            mesh=split,
            in_specs=(P(grid, "x"), P("x", None), P(), P()),
            out_specs=P((*grid, "x"), None),
            check_vma=False,
        )(fields, start_local, start_pair, start_root)

    return whole
```

```python
import functools

import jax
import jax.numpy as jnp
from jax import lax
from jax.experimental import pallas as pl
from jax.experimental.pallas import tpu as pltpu
from jax.sharding import Mesh
from jax.sharding import PartitionSpec as P

POWER = 2
NEWTON = 8
RANK = 128
NZ, NY, NC, NX = 8, 4, 2, 4
ROW = NY * NC
SHEET = NZ * NY
PLANE = NX * ROW
EARLY = 5
PIECE = 192
MESH = pl.DeviceIdType.MESH
F32 = jnp.float32
BF16 = jnp.bfloat16


def product(a, b):
    return jnp.dot(a, b, preferred_element_type=F32)


def product_t(a, b):
    return lax.dot_general(a, b, (((0,), (0,)), ((), ())), preferred_element_type=F32)


def halves(a):
    high = a.astype(BF16)
    return high, (a - high.astype(F32)).astype(BF16)


def three_products(a, b, dims):
    (a_high, a_low), (b_high, b_low) = halves(a), halves(b)
    (a_dim,), (b_dim,) = dims
    left = jnp.concatenate([a_high, a_high, a_low], axis=a_dim)
    right = jnp.concatenate([b_high, b_low, b_high], axis=b_dim)
    return lax.dot_general(left, right, (dims, ((), ())), preferred_element_type=F32)


def power_steps(grams, bases):
    steps = [three_products(basis, gram, ((1,), (0,))) for gram, basis in zip(grams, bases)]
    flat = [w * (1.0 / jnp.sqrt(jnp.sum(w * w) + 1e-06)) for w in steps]
    for _ in range(NEWTON):
        inner = [three_products(w, w, ((1,), (1,))) for w in flat]
        flat = [1.5 * w - 0.5 * three_products(s, w, ((1,), (0,))) for s, w in zip(inner, flat)]
    return flat


def turned(gram, left, right):
    high, low = halves(gram)
    middle = product(jnp.concatenate([high, low], axis=1), jnp.concatenate([right, right], axis=0))
    high, low = halves(middle)
    return product_t(jnp.concatenate([left, left], axis=0), jnp.concatenate([high, low], axis=0))


def body(
    inverse_count,
    fields, start_local, start_pair, start_root,
    out,
    f, s_local, s_pair, s_root,
    gram, got_c, kept_y, got_y, part_a, got_a, mine_a, col,
    raw, rot_all, leaves, sent_leaf, diag, diag_part, diag_all,
    pair_part, got_p, mine_p, zs_p, pair_all, piece_p,
    cross_part, got_x, mine_x, zs_x, cross_all, piece_x,
    load_sem, start_sem, near, far, c_sem, y_sem, a_sem, b_sem, d_sem, raw_sem, rot_sem, leaf_sem, e_sem, g_sem, p_sem, x_sem,
):
    z, y, c, x = (lax.axis_index(name) for name in ("z", "y", "c", "x"))
    j = y * NC + c
    m = y * NZ + z
    t = x * ROW + j
    quarter = f.shape[0] // NX
    early = raw.shape[1]
    late = quarter - early
    pending = []

    def send(src, dst, sems, **where):
        pltpu.make_async_remote_copy(
            src_ref=src, dst_ref=dst, send_sem=sems.at[0], recv_sem=sems.at[1],
            device_id=where, device_id_type=MESH,
        ).start()

    def await_bytes(ref, sem):
        pltpu.make_async_copy(ref, ref, sem).wait()

    def arrived(ref, sems):
        pending.append((ref, sems.at[0]))
        await_bytes(ref, sems.at[1])

    def greet(**where):
        pl.semaphore_signal(pltpu.get_barrier_semaphore(), inc=1, device_id=where, device_id_type=MESH)

    def away(index, k, size):
        step = (k + 1) // 2
        return lax.rem(index + size // 2 + jnp.where(lax.rem(k, 2) == 1, size - step, step), size)

    def in_row(k):
        peer_y, peer_c = away(y, k // NC, NY), away(c, lax.rem(k, NC), NC)
        return peer_y * NC + peer_c, dict(y=peer_y, c=peer_c)

    def in_sheet(k):
        return dict(z=away(z, k // NY, NZ), y=away(y, lax.rem(k, NY), NY))

    def in_plane(k):
        peer_x = away(x, k // ROW, NX)
        peer, where = in_row(lax.rem(k, ROW))
        return peer_x * ROW + peer, dict(x=peer_x, **where)

    @pl.loop(0, NZ - 1)
    def _(k):
        greet(z=away(z, k, NZ), c=1)

    loads = []
    for k in range(NX):
        rows = pl.ds(k * quarter, quarter)
        loads.append(pltpu.make_async_copy(fields.at[rows], f.at[rows], load_sem.at[k]))
    own_early = pl.ds(pl.multiple_of(x * quarter, quarter), early)
    loads.append(pltpu.make_async_copy(fields.at[own_early], raw.at[x], load_sem.at[NX]))
    for k, (src, dst) in enumerate([(start_local, s_local), (start_pair, s_pair), (start_root, s_root)]):
        loads.append(pltpu.make_async_copy(src, dst, start_sem.at[k]))
    for load in loads:
        load.start()

    for k in range(NX - 1):
        greet(x=away(x, k, NX), c=0)
    for k in range(NY - 1):
        greet(y=away(y, k, NY), c=0)

    @pl.when(c == 1)
    def _():
        greet(c=0)

    total = None
    for k in range(NX):
        loads[k].wait()
        part = f[pl.ds(k * quarter, quarter)]
        term = product_t(part, part)
        total = term if total is None else total + term
    gram[...] = total

    @pl.when(c == 0)
    def _():
        pl.semaphore_wait(pltpu.get_barrier_semaphore(), NC * (NX - 1 + NY - 1) + 1)
        pl.semaphore_signal(near, inc=1, device_id=dict(c=1), device_id_type=MESH)

    @pl.when(c == 1)
    def _():
        pl.semaphore_wait(near, 1)

    half = gram.shape[0] // NC
    send(gram.at[pl.ds(pl.multiple_of((1 - c) * half, 8), half)], got_c, c_sem, c=1 - c)

    @pl.loop(0, early // PIECE)
    def _(k):
        for d in (2, 1, 3):
            peer = lax.rem(x + d, NX)
            rows = pl.ds(pl.multiple_of(peer * quarter + k * PIECE, PIECE), PIECE)
            send(f.at[rows], raw.at[x, pl.ds(pl.multiple_of(k * PIECE, PIECE), PIECE)], raw_sem, x=peer)

    arrived(got_c, c_sem)
    kept = gram[pl.ds(pl.multiple_of(c * half, 8), half)] + got_c[...]
    kept_y[...] = kept

    strip = half // NY
    for k in range(NY - 1):
        peer = away(y, k, NY)
        send(kept_y.at[pl.ds(pl.multiple_of(peer * strip, 8), strip)], got_y.at[k], y_sem, y=peer)
    arrived(got_y, y_sem)
    sums = kept_y[pl.ds(pl.multiple_of(y * strip, 8), strip)] + got_y[...].sum(axis=0)
    for n in range(NZ):
        r, s = 8 * (n // 2), 128 * (n % 2)
        part_a[n] = sums[r:r + 8, s:s + 128]

    @pl.when(c == 1)
    def _():
        pl.semaphore_wait(pltpu.get_barrier_semaphore(), NC * (NZ - 1))
        pl.semaphore_signal(far, inc=1, device_id=dict(c=0), device_id_type=MESH)

    @pl.when(c == 0)
    def _():
        pl.semaphore_wait(far, 1)

    @pl.loop(0, NZ - 1)
    def _(k):
        peer = away(z, k, NZ)
        send(part_a.at[peer], got_a.at[k], a_sem, z=peer)

    arrived(got_a, a_sem)
    tile = (part_a[z] + got_a[...].sum(axis=0)) * inverse_count
    mine_a[...] = tile
    col[c, m] = tile

    @pl.loop(0, SHEET - 1)
    def _(d):
        send(mine_a, col.at[c, m], b_sem, **in_sheet(d))

    arrived(col.at[0, pl.ds(0, SHEET - 1)], b_sem)
    send(col.at[c], col.at[c], d_sem, c=1 - c)
    arrived(col.at[0], d_sem)
    whole = jnp.concatenate(
        [
            jnp.concatenate([col[n, 2 * k], col[n, 2 * k + 1]], axis=1)
            for n in range(NC)
            for k in range(SHEET // 2)
        ],
        axis=0,
    )
    for load in loads[NX:]:
        load.wait()
    bases = [s_local[...].T]
    for _ in range(POWER):
        bases = power_steps([whole], bases)
    rotation = bases[0].T.astype(BF16)

    rot_all[x] = rotation
    for d in (2, 1, 3):
        send(rot_all.at[x], rot_all.at[x], rot_sem, x=lax.rem(x + d, NX))
    for n, d in enumerate((2, 1, 3)):
        peer = lax.rem(x + d, NX)
        rows = pl.ds(pl.multiple_of(peer * quarter + early, PIECE), late)
        sent_leaf[n] = product(f[rows], rotation).astype(BF16)
        send(sent_leaf.at[n], leaves.at[x, pl.ds(early, late)], leaf_sem, x=peer)

    diag[...] = turned(whole, rotation, rotation)
    part16 = pl.ds(pl.multiple_of(j * 16, 16), 16)
    diag_part[x] = diag[part16]
    for d in (1, 2, 3):
        send(diag.at[part16], diag_part.at[x], e_sem, x=lax.rem(x + d, NX))

    own_late = pl.ds(pl.multiple_of(x * quarter + early, PIECE), late)
    leaves[x, pl.ds(early, late)] = product(f[own_late], rotation).astype(BF16)

    leaves[x, pl.ds(0, early)] = product(raw[x], rotation).astype(BF16)
    arrived(raw.at[pl.ds(0, NX - 1)], raw_sem)
    arrived(rot_all.at[pl.ds(0, NX - 1)], rot_sem)
    for d in (1, 2, 3):
        b = lax.rem(x + d, NX)
        leaves[b, pl.ds(0, early)] = product(raw[b], rot_all[b]).astype(BF16)

    def joined(n, rows):
        return jnp.concatenate([leaves[2 * n, rows], leaves[2 * n + 1, rows]], axis=1)

    first_rows, last_rows, all_rows = slice(0, early), slice(early, quarter), slice(0, quarter)
    for n in range(2):
        pair_part[128 * n:128 * n + 128] = product_t(leaves[2 * n, first_rows], leaves[2 * n + 1, first_rows])
    arrived(leaves.at[pl.ds(0, NX - 1), pl.ds(early, late)], leaf_sem)
    for n in range(2):
        pair_part[128 * n:128 * n + 128] += product_t(leaves[2 * n, last_rows], leaves[2 * n + 1, last_rows])

    @pl.loop(0, PLANE - 1)
    def _(d):
        peer, where = in_plane(d)
        send(pair_part.at[pl.ds(pl.multiple_of(peer * 8, 8), 8)], got_p.at[d], p_sem.at[0], **where)

    cross_part[...] = product_t(joined(0, all_rows), joined(1, all_rows))

    @pl.loop(0, PLANE - 1)
    def _(d):
        peer, where = in_plane(d)
        send(cross_part.at[pl.ds(pl.multiple_of(peer * 8, 8), 8)], got_x.at[d], x_sem.at[0], **where)

    arrived(diag_part.at[pl.ds(0, NX - 1)], e_sem)
    diag_all[j] = diag_part[...]

    @pl.loop(0, ROW - 1)
    def _(d):
        send(diag_part, diag_all.at[j], g_sem, **in_row(d)[1])

    my8 = pl.ds(pl.multiple_of(t * 8, 8), 8)

    def over_z(got, part, mine, zs, sems):
        arrived(got, sems.at[0])
        value = part[my8] + got[...].sum(axis=0)
        mine[...] = value
        zs[z] = value

        @pl.loop(0, NZ - 1)
        def _(d):
            send(mine, zs.at[z], sems.at[1], z=away(z, d, NZ))

    def to_plane(zs, piece, whole_ref, sems):
        arrived(zs.at[pl.ds(0, NZ - 1)], sems.at[1])
        value = zs[...].sum(axis=0) * inverse_count
        piece[...] = value
        whole_ref[my8] = value

        @pl.loop(0, PLANE - 1)
        def _(d):
            send(piece, whole_ref.at[my8], sems.at[2], **in_plane(d)[1])

    def from_plane(whole_ref, sems):
        arrived(whole_ref.at[pl.ds(0, 8 * (PLANE - 1))], sems.at[2])

    over_z(got_p, pair_part, mine_p, zs_p, p_sem)
    over_z(got_x, cross_part, mine_x, zs_x, x_sem)
    to_plane(zs_p, piece_p, pair_all, p_sem)
    to_plane(zs_x, piece_x, cross_all, x_sem)
    arrived(diag_all.at[pl.ds(0, ROW - 1)], g_sem)
    diags = [jnp.concatenate([diag_all[n, b] for n in range(ROW)], axis=0) for b in range(NX)]
    from_plane(pair_all, p_sem)

    def pair_gram(n):
        block = pair_all[128 * n:128 * n + 128]
        top = jnp.concatenate([diags[2 * n], block], axis=1)
        low = jnp.concatenate([block.T, diags[2 * n + 1]], axis=1)
        return jnp.concatenate([top, low], axis=0)

    grams = [pair_gram(0), pair_gram(1)]
    bases = power_steps(grams, [s_pair[n].T for n in range(2)])
    bases = power_steps(grams, bases)
    rotations = [basis.T.astype(BF16) for basis in bases]
    first = turned(grams[0], rotations[0], rotations[0])
    second = turned(grams[1], rotations[1], rotations[1])
    from_plane(cross_all, x_sem)
    mixed = turned(cross_all[...], rotations[0], rotations[1])
    root_gram = jnp.concatenate(
        [jnp.concatenate([first, mixed], axis=1), jnp.concatenate([mixed.T, second], axis=1)], axis=0
    )
    branch = jnp.concatenate(
        [product(joined(n, all_rows), rotations[n]).astype(BF16) for n in range(2)], axis=1
    )
    bases = [s_root[...].T]
    for _ in range(POWER):
        bases = power_steps([root_gram], bases)
    out[...] = product(branch, bases[0].T.astype(BF16)).astype(BF16)

    for ref, sem in pending:
        await_bytes(ref, sem)


def on_device(points, fields, start_local, start_pair, start_root):
    rows, snaps = fields.shape
    vmem = pltpu.VMEM
    dma = pltpu.SemaphoreType.DMA
    quarter = rows // NX
    early = EARLY * quarter // 8
    scratch = [
        vmem((rows, snaps), BF16), vmem(start_local.shape, F32), vmem(start_pair.shape, F32), vmem(start_root.shape, F32),
        vmem((snaps, snaps), F32), vmem((snaps // NC, snaps), F32), vmem((snaps // NC, snaps), F32),
        vmem((NY - 1, snaps // NC // NY, snaps), F32), vmem((NZ, 8, 128), F32), vmem((NZ - 1, 8, 128), F32), vmem((8, 128), F32), vmem((NC, SHEET, 8, 128), F32),
        vmem((NX, early, snaps), BF16), vmem((NX, snaps, RANK), BF16),
        vmem((NX, quarter, RANK), BF16), vmem((NX - 1, quarter - early, RANK), BF16), vmem((RANK, RANK), F32),
        vmem((NX, 16, RANK), F32), vmem((ROW, NX, 16, RANK), F32),
        vmem((256, 128), F32), vmem((PLANE - 1, 8, 128), F32), vmem((8, 128), F32), vmem((NZ, 8, 128), F32),
        vmem((256, 128), F32), vmem((8, 128), F32),
        vmem((256, 256), F32), vmem((PLANE - 1, 8, 256), F32), vmem((8, 256), F32), vmem((NZ, 8, 256), F32),
        vmem((256, 256), F32), vmem((8, 256), F32),
        dma((NX + 1,)), dma((3,)), *[pltpu.SemaphoreType.REGULAR] * 2, *[dma((2,))] * 10, dma((3, 2)), dma((3, 2)),
    ]
    anywhere = pl.BlockSpec(memory_space=pltpu.HBM)
    return pl.pallas_call(
        functools.partial(body, 1.0 / points),
        out_shape=jax.ShapeDtypeStruct((quarter, RANK), BF16),
        in_specs=[anywhere] * 4,
        out_specs=pl.BlockSpec(memory_space=pltpu.VMEM),
        scratch_shapes=scratch,
        compiler_params=pltpu.CompilerParams(
            collective_id=0, has_side_effects=True, vmem_limit_bytes=48 * 2**20
        ),
        name="snapshot_modes",
    )(*(pltpu.with_memory_space_constraint(a, pltpu.HBM) for a in (fields, start_local, start_pair, start_root)))


def solution(mesh):
    split = Mesh(mesh.devices.reshape(NZ, NY, NC, mesh.shape["snap"]), ("z", "y", "c", "x"))
    grid = ("z", "y", "c")

    def whole(fields, start_local, start_pair, start_root):
        return jax.shard_map(
            functools.partial(on_device, fields.shape[0]),
            mesh=split,
            in_specs=(P(grid, "x"), P("x", None), P(), P()),
            out_specs=P((*grid, "x"), None),
            check_vma=False,
        )(fields, start_local, start_pair, start_root)

    return whole
```
